32 devices in a mesh: ctx: 8 (over z, y), fsdp: 4 (over x, core).
Axes of the slice: x: 2, y: 2, z: 4, core: 2. Of those that a mesh axis runs over, the one named last changes fastest.
Arguments:
- hidden: bfloat16 [4096, 4096], P('ctx', 'fsdp'), may hold values from -6 to 6
- w_in: bfloat16 [768, 4096], P('ctx', 'fsdp'), may hold values from -1.25 to 1.25
- decay: float32 [4, 4096], P(None, 'ctx'), may hold values from 0.999 to 1
- norm_gain: float32 [256], replicated, may hold values from 0.1 to 1.9
- w_out: bfloat16 [256, 4096], P('ctx', 'fsdp'), may hold values from -0.75 to 0.75
- grad_out: bfloat16 [4096, 4096], P('ctx', 'fsdp'), may hold values from -6 to 6
Outputs:
- grad_hidden: bfloat16 [4096, 4096], P('ctx', 'fsdp')
- grad_w_in: float32 [768, 4096], P('ctx', 'fsdp')
- grad_w_out: float32 [256, 4096], P('ctx', 'fsdp')
The draws below stay inside these ranges and needn't reach their ends.
All inputs are finite; a program needn't handle non-finite values.
Results may differ from the reference program's by a relative error of at most 0.0075.
Values may be sent and summed in bfloat16 or wider, within the bound.
A program may use at most 128 MiB of HBM per device.

```python
import math
import jax
import jax.numpy as jnp
from jax import lax

D = 4096
H = 4
P_SIZE = 64
N = 128
TOK_DEV = 512
HP = 256
CIN = 768
TOKENS = 4096


def draw_w_in(key, part):
    first, second = jax.random.split(key)
    scales = jnp.exp(jax.random.uniform(first, (CIN, 1), jnp.float32, math.log(0.1), math.log(10.0)))
    ramp = jnp.arange(D, dtype=jnp.float32)[None, :] / (D - 1)
    entries = jnp.clip(jax.random.normal(second, (CIN, D), jnp.float32), -4.0, 4.0)
    profile = jnp.exp(math.log(0.6) + ramp * (math.log(1.8) - math.log(0.6)))
    return (entries * scales * profile / math.sqrt(D)).astype(jnp.bfloat16)


def draw_w_out(key, part):
    first, second = jax.random.split(key)
    scales = jnp.exp(jax.random.uniform(first, (1, D), jnp.float32, math.log(0.3), math.log(3.0)))
    entries = jnp.clip(jax.random.normal(second, (HP, D), jnp.float32), -4.0, 4.0)
    return (entries * scales / math.sqrt(HP)).astype(jnp.bfloat16)


def draw_decay(key, part):
    first, second, third, fourth = jax.random.split(key, 4)
    order = jax.random.permutation(first, H)
    slow_base = jnp.minimum(jax.random.uniform(second, (H, 1), jnp.float32, 0.2, 0.8) * math.log(10.0) / TOKENS, 0.00025)
    fast_base = jnp.exp(jax.random.uniform(third, (H, 1), jnp.float32, math.log(6e-05), math.log(0.00025)))
    rates = jnp.where(order[:, None] < H // 2, slow_base, fast_base)
    blocks = TOKENS // TOK_DEV
    block_factor = jnp.exp(jax.random.uniform(fourth, (H, blocks, 1), jnp.float32, math.log(0.25), math.log(4.0)))
    jitter = jnp.broadcast_to(block_factor, (H, blocks, TOK_DEV)).reshape(H, TOKENS)
    per_token = jnp.minimum(rates * jitter, 0.001)
    return jnp.exp(-per_token).astype(jnp.float32)


def block_levels(own_key, extent, cuts, low, top_value):
    loudness = 1.0
    for axis_at, parts in cuts:
        heights = jax.random.uniform(jax.random.fold_in(jax.random.fold_in(own_key, 6), axis_at), (parts,), jnp.float32, low / len(cuts), top_value / len(cuts))
        loudness = loudness * jnp.repeat(jnp.exp(heights), extent[axis_at] // parts).reshape((-1,) + (1,) * (len(extent) - 1 - axis_at))
    return loudness


def gaussian(own_key, extent, width, reach, cuts=(), kind=jnp.bfloat16):
    drawn = width * jax.random.normal(own_key, extent, jnp.float32)
    if cuts:
        drawn = drawn * block_levels(own_key, extent, cuts, -0.22, 0.18)
    return jnp.clip(drawn, -reach, reach).astype(kind)


def setup_inputs(seed: int = 0) -> dict:
    key_list = jax.random.split(jax.random.key(seed), 7)
    hidden = gaussian(key_list[0], (TOKENS, D), 1.0, 6.0, ((0, 8), (1, 4)))
    w_in = draw_w_in(jax.random.fold_in(key_list[6], 71), 0)
    decay = draw_decay(jax.random.fold_in(key_list[6], 71), 0)
    norm_gain = jnp.clip(1.0 + 0.18 * jax.random.normal(key_list[3], (HP,), jnp.float32), 0.1, 1.9)
    w_out = draw_w_out(jax.random.fold_in(key_list[6], 71), 0)
    grad_out = gaussian(key_list[5], (TOKENS, D), 1.0, 6.0, ((0, 8), (1, 4)))
    return {"hidden": hidden, "w_in": w_in, "decay": decay, "norm_gain": norm_gain, "w_out": w_out, "grad_out": grad_out}


highest = lax.Precision.HIGHEST
clip_output = 10.0

def split_columns(projection):
    return (projection[:, :HP], projection[:, HP:2 * HP], projection[:, 2 * HP:2 * HP + N], projection[:, 2 * HP + N:])

def intra_block(x_part, b_part, c_part, log_decay):
    length = x_part.shape[0]
    cum_decay = jnp.cumsum(log_decay, axis=1)
    x_heads = x_part.reshape(length, H, P_SIZE)
    causal = jnp.arange(length)[:, None] >= jnp.arange(length)[None, :]
    gaps = jnp.where(causal[None], cum_decay[:, :, None] - cum_decay[:, None, :], 0.0)
    weights = jnp.where(causal[None], jnp.exp(gaps), 0.0)
    scores = jnp.dot(c_part, b_part.T, precision=highest)
    mixed = weights * scores[None]
    y_intra = jnp.einsum('hts,shp->thp', mixed, x_heads, precision=highest).reshape(length, H * P_SIZE)
    tail = jnp.exp(cum_decay[:, -1:] - cum_decay)
    weighted = x_heads * tail.T[:, :, None]
    state_part = jnp.einsum('shp,sn->hpn', weighted, b_part, precision=highest)
    return (y_intra, state_part, cum_decay)

def finish_block(gate_part, y_intra, c_part, start_state, cum_decay, norm_gain):
    length = c_part.shape[0]
    carried = jnp.einsum('hpn,tn->thp', start_state, c_part, precision=highest)
    carried = carried * jnp.exp(cum_decay).T[:, :, None]
    y_full = y_intra + carried.reshape(length, H * P_SIZE)
    gated = y_full * jax.nn.silu(gate_part)
    factor = lax.rsqrt(lax.optimization_barrier(jnp.mean(gated * gated, axis=-1, keepdims=True)) + 1e-05)
    return gated * factor * norm_gain

def mixer(projection, log_decay, norm_gain):
    blocks = TOKENS // TOK_DEV
    stacked = projection.reshape(blocks, TOK_DEV, CIN)
    decays = log_decay.reshape(H, blocks, TOK_DEV).transpose(1, 0, 2)

    def advance(start_state, inputs):
        block, block_decay = inputs
        gate_part, x_part, b_part, c_part = split_columns(block)
        y_intra, state_part, cum_decay = intra_block(x_part, b_part, c_part, block_decay)
        normed = finish_block(gate_part, y_intra, c_part, start_state, cum_decay, norm_gain)
        end_state = jnp.exp(cum_decay[:, -1])[:, None, None] * start_state + state_part
        return (end_state, normed)
    _, normed = lax.scan(advance, jnp.zeros((H, P_SIZE, N), jnp.float32), (stacked, decays))
    return normed.reshape(TOKENS, HP)

def reference(hidden, w_in, decay, norm_gain, w_out, grad_out):
    clip_input = math.sqrt(D)
    projection = jnp.dot(hidden, w_in.T, preferred_element_type=jnp.float32)
    grad_normed = jnp.dot(grad_out, w_out.T, preferred_element_type=jnp.float32)
    log_decay = jnp.log(decay)
    normed, pullback = jax.vjp(lambda value: mixer(value, log_decay, norm_gain), projection)
    grad_projection = pullback(grad_normed)[0].astype(jnp.bfloat16)
    normed_rounded = normed.astype(jnp.bfloat16)
    grad_hidden = jnp.dot(grad_projection, w_in, preferred_element_type=jnp.float32).astype(jnp.bfloat16)
    root_tokens = math.sqrt(TOKENS)
    raw_in = jnp.dot(grad_projection.T, hidden, preferred_element_type=jnp.float32) / root_tokens
    raw_out = jnp.dot(normed_rounded.T, grad_out, preferred_element_type=jnp.float32) / root_tokens
    weight_in = jnp.sqrt(lax.optimization_barrier(jnp.sum(jnp.square(w_in.astype(jnp.float32)), axis=1)))
    norm_in = jnp.sqrt(lax.optimization_barrier(jnp.sum(raw_in * raw_in, axis=1)))
    factor_in = jnp.minimum(1.0, clip_input * jnp.maximum(weight_in, 0.001) / jnp.maximum(norm_in, 1e-06))
    weight_out = jnp.sqrt(lax.optimization_barrier(jnp.sum(jnp.square(w_out.astype(jnp.float32)), axis=0)))
    norm_out = jnp.sqrt(lax.optimization_barrier(jnp.sum(raw_out * raw_out, axis=0)))
    factor_out = jnp.minimum(1.0, clip_output * jnp.maximum(weight_out, 0.001) / jnp.maximum(norm_out, 1e-06))
    return (grad_hidden, raw_in * factor_in[:, None], raw_out * factor_out[None, :])
```

```python
import functools
import math

import jax
import jax.numpy as jnp
from jax import lax
from jax.experimental import pallas as pl
from jax.experimental.pallas import tpu as pltpu
from jax.sharding import PartitionSpec as P

D = 4096
H = 4
P_SIZE = 64
N = 128
HP = 256


highest = lax.Precision.HIGHEST
clip_output = 10.0


def prefix(x, axis, combine, identity):
    count, index = (lax.axis_size(axis), lax.axis_index(axis))
    everything = jax.tree.map(lambda part: lax.all_gather(part, axis), x)
    start = jax.tree.map(
        lambda part, zero: jnp.broadcast_to(jnp.asarray(zero, part.dtype), part.shape), x, identity
    )

    def step(k, before):
        reached = k < index
        new = combine(before, jax.tree.map(lambda part: part[k], everything))
        return jax.tree.map(lambda a, b: jnp.where(reached, a, b), new, before)

    return lax.fori_loop(0, count, step, start)


def entering(x, axis, join, neutral):
    count = lax.axis_size(axis)
    place = lax.axis_index(axis)
    ahead = count - 1 - place
    gathered = jax.tree.map(
        lambda a, kind: lax.all_gather(a.astype(kind), axis),
        x,
        jax.tree.map(lambda a: jnp.bfloat16 if a.dtype == jnp.float32 else a.dtype, x),
    )
    state = jax.tree.map(lambda a, e: jnp.zeros_like(a) + jnp.asarray(e, a.dtype), x, neutral)

    def one(step, state):
        source = count - 1 - step
        return join(
            state,
            jax.tree.map(
                lambda a, own: lax.dynamic_index_in_dim(a, source, 0, False).astype(own.dtype),
                gathered,
                x,
            ),
        )

    return lax.fori_loop(0, ahead, one, state)


def split_columns(projection):
    return (
        projection[:, :HP],
        projection[:, HP : 2 * HP],
        projection[:, 2 * HP : 2 * HP + N],
        projection[:, 2 * HP + N :],
    )


def intra_block(x_part, b_part, c_part, log_decay):
    length = x_part.shape[0]
    cum_decay = jnp.cumsum(log_decay, axis=1)
    x_heads = x_part.reshape(length, H, P_SIZE)
    causal = jnp.arange(length)[:, None] >= jnp.arange(length)[None, :]
    gaps = jnp.where(causal[None], cum_decay[:, :, None] - cum_decay[:, None, :], 0.0)
    weights = jnp.where(causal[None], jnp.exp(gaps), 0.0)
    scores = jnp.dot(c_part, b_part.T, precision=highest)
    mixed = weights * scores[None]
    y_intra = jnp.einsum("hts,shp->thp", mixed, x_heads, precision=highest).reshape(
        length, H * P_SIZE
    )
    tail = jnp.exp(cum_decay[:, -1:] - cum_decay)
    weighted = x_heads * tail.T[:, :, None]
    state_part = jnp.einsum("shp,sn->hpn", weighted, b_part, precision=highest)
    return (y_intra, state_part, cum_decay)


def finish_block(gate_part, y_intra, c_part, start_state, cum_decay, norm_gain):
    length = c_part.shape[0]
    carried = jnp.einsum("hpn,tn->thp", start_state, c_part, precision=highest)
    carried = carried * jnp.exp(cum_decay).T[:, :, None]
    y_full = y_intra + carried.reshape(length, H * P_SIZE)
    gated = y_full * jax.nn.silu(gate_part)
    factor = lax.rsqrt(jnp.mean(gated * gated, axis=-1, keepdims=True) + 1e-05)
    return gated * factor * norm_gain


def carry_states(earlier, later):
    return (earlier[0] * later[0], later[0] * earlier[1] + later[1])


def carry_adjoint(earlier, later):
    return (earlier[0] * later[0], later[1] + later[0] * earlier[1])


def local(hidden, w_in, decay, norm_gain, w_out, grad_out):
    clip_input = math.sqrt(D)
    tok_rows = hidden.shape[0]
    root_tokens = math.sqrt(tok_rows * lax.axis_size("ctx"))
    contract_last = (((1,), (1,)), ((), ()))
    contract_first = (((0,), (0,)), ((), ()))
    partial_proj = lax.dot_general(
        hidden,
        lax.all_gather(w_in, "ctx", axis=0, tiled=True),
        contract_last,
        preferred_element_type=jnp.float32,
    )
    slab_out = lax.all_gather(w_out, "ctx", axis=0, tiled=True)
    partial_grad = lax.dot_general(
        grad_out, slab_out, contract_last, preferred_element_type=jnp.float32
    )
    projection, grad_normed = lax.psum((partial_proj, partial_grad), "fsdp")
    log_decay = jnp.log(decay)
    gate_part, x_part, b_part, c_part = split_columns(projection)

    def intra_only(x_value, b_value, c_value):
        return intra_block(x_value, b_value, c_value, log_decay)

    (y_intra, state_part, cum_decay), intra_pull = jax.vjp(intra_only, x_part, b_part, c_part)
    decay_total = jnp.exp(cum_decay[:, -1])[:, None, None]
    identity = (jnp.ones_like(decay_total), jnp.zeros_like(state_part))
    _, start_state = prefix((decay_total, state_part), "ctx", carry_states, identity)

    def finish_only(gate_value, intra_value, c_value, state_value):
        return finish_block(gate_value, intra_value, c_value, state_value, cum_decay, norm_gain)

    normed, finish_pull = jax.vjp(finish_only, gate_part, y_intra, c_part, start_state)
    grad_gate, grad_intra, grad_c_late, grad_start = finish_pull(grad_normed)
    _, grad_end = entering((decay_total, grad_start), "ctx", carry_adjoint, identity)
    grad_x, grad_b, grad_c_early = intra_pull((grad_intra, grad_end, jnp.zeros_like(cum_decay)))
    grad_projection = jnp.concatenate(
        [grad_gate, grad_x, grad_b, grad_c_early + grad_c_late], axis=1
    ).astype(jnp.bfloat16)
    columns = grad_projection
    grad_hidden = jnp.dot(
        columns, lax.all_gather(w_in, "ctx", axis=0, tiled=True), preferred_element_type=jnp.float32
    )
    columns = grad_projection
    raw_in = (
        lax.psum_scatter(
            lax.dot_general(columns, hidden, contract_first, preferred_element_type=jnp.float32),
            "ctx",
            scatter_dimension=0,
            tiled=True,
        )
        / root_tokens
    )
    weight_square = jnp.sum(jnp.square(w_in.astype(jnp.float32)), axis=1)
    weight_in, grad_in = lax.psum((weight_square, jnp.sum(raw_in * raw_in, axis=1)), "fsdp")
    factor_in = jnp.minimum(
        1.0,
        clip_input
        * jnp.maximum(jnp.sqrt(weight_in), 0.001)
        / jnp.maximum(jnp.sqrt(grad_in), 1e-06),
    )
    normed_rounded = normed.astype(jnp.bfloat16)
    weight_out = jnp.sqrt(jnp.sum(jnp.square(slab_out.astype(jnp.float32)), axis=0))
    raw_out = (
        lax.psum_scatter(
            lax.dot_general(
                normed_rounded, grad_out, contract_first, preferred_element_type=jnp.float32
            ),
            "ctx",
            scatter_dimension=0,
            tiled=True,
        )
        / root_tokens
    )
    grad_square = lax.psum(jnp.sum(raw_out * raw_out, axis=0), "ctx")
    factor_out = jnp.minimum(
        1.0,
        clip_output * jnp.maximum(weight_out, 0.001) / jnp.maximum(jnp.sqrt(grad_square), 1e-06),
    )
    return (
        grad_hidden.astype(jnp.bfloat16),
        raw_in * factor_in[:, None],
        raw_out * factor_out[None, :],
    )


NN = (((1,), (0,)), ((), ()))
NT = (((1,), (1,)), ((), ()))
TN = (((0,), (0,)), ((), ()))
MESH = pl.DeviceIdType.MESH
f32 = jnp.float32
bf16 = jnp.bfloat16
EPS = 1e-05


def split(a):
    hi = a.astype(bf16)
    return hi, (a - hi.astype(f32)).astype(bf16)


def dot1(a, b, dims):
    return lax.dot_general(a, b, dims, preferred_element_type=f32)


def dot3(a, b, dims):
    return dot1(a[0], b[0], dims) + (dot1(a[0], b[1], dims) + dot1(a[1], b[0], dims))


def transposed(pair):
    return pair[0].T, pair[1].T


def fused(
    n, fs, root_tokens, clip_input,
    hid_any, win_ref, dec_any, gain_any, wout_ref, gout_any,
    gh_any, gwi_any, gwo_any,
    hidT, goutT, wi_all, wo_all, pT, buf, core_in, x_out, x_in, c_in, e_out, e_all,
    e_ref, st_out, st_all, s0_ref, ad_out, ad_all, g_ref,
    ro, ob1, ob1r, ob2, ob2r, gp, ri, ib1, ib1r, ib2, ib2r,
    nin_out, nin_all, nout_out, nout_all,
    g_send, g_recv, p_send, p_recv, s_send, s_recv, o_send, o_recv, i_send, i_recv,
    n_send, n_recv, tmp, hid_ref, gout_ref, dec_ref, gain_ref, gh_ref, gwi_ref, gwo_ref, l_sem,
):
    c = lax.axis_index("ctx")
    f = lax.axis_index("fsdp")
    outer = n // 2
    z, y = c // 2, lax.rem(c, 2)
    yn = c + 1 - 2 * y
    core = lax.rem(f, 2)
    fcore = f + 1 - 2 * core
    fx = lax.rem(f + fs // 2, fs)
    rows_in, d = win_ref.shape
    rows_out = wout_ref.shape[0]
    tok = hid_any.shape[0]
    cin, hp = rows_in * n, rows_out * n
    nst = (cin - 2 * hp) // 2
    hpf = hp // fs

    def copy(src, dst, ssem, rsem, dev):
        return pltpu.make_async_remote_copy(
            src_ref=src, dst_ref=dst, send_sem=ssem, recv_sem=rsem,
            device_id=dev, device_id_type=MESH)

    sent = []

    def go(*args, when=None):
        if when is None:
            copy(*args).start()
        else:
            pl.when(when)(lambda: copy(*args).start())
        sent.append((when, args))

    def arrive(*args, when=None):
        if when is None:
            copy(*args).wait_recv()
        else:
            pl.when(when)(lambda: copy(*args).wait_recv())

    local = [
        pltpu.make_async_copy(src, dst, l_sem.at[i])
        for i, (src, dst) in enumerate((
            (hid_any, hid_ref), (win_ref, wi_all.at[c]), (gout_any, gout_ref),
            (wout_ref, wo_all.at[c]), (dec_any, dec_ref), (gain_any, gain_ref)))
    ]
    for each in local:
        each.start()

    barrier = pltpu.get_barrier_semaphore()
    for k in range(1, n):
        pl.semaphore_signal(barrier, inc=1, device_id=(lax.rem(c + k, n), f), device_id_type=MESH)
    for k in range(1, fs):
        pl.semaphore_signal(barrier, inc=1, device_id=(c, lax.rem(f + k, fs)), device_id_type=MESH)
    pl.semaphore_wait(barrier, n + fs - 2)

    both = ((win_ref, wi_all), (wout_ref, wo_all))
    up = jnp.minimum(z + 1, outer - 1) * 2 + y
    down = jnp.maximum(z - 1, 0) * 2 + y
    order = [1, outer - 1] + list(range(2, outer - 1))
    for a, (src, dst) in enumerate(both):
        go(src, dst.at[c], g_send.at[0, a, c], g_recv.at[a, c], (up, f), when=z < outer - 1)
        go(src, dst.at[c], g_send.at[1, a, c], g_recv.at[a, c], (down, f), when=z > 0)
        go(src, dst.at[c], g_send.at[2, a, c], g_recv.at[a, c], (yn, f))
    for each in local:
        each.wait()
    hidT[...] = hid_ref[...].T
    goutT[...] = gout_ref[...].T

    decay = dec_ref[...]
    lane = lax.broadcasted_iota(jnp.int32, decay.shape, 1)
    shift = 1
    while shift < tok:
        decay = decay * jnp.where(lane >= shift, pltpu.roll(decay, shift, 1), 1.0)
        shift *= 2
    heads = decay.shape[0]
    for h in range(heads):
        e_ref[h * (hp // heads) : (h + 1) * (hp // heads), :] = jnp.broadcast_to(
            decay[h : h + 1], (hp // heads, tok))

    e_out[...] = jnp.broadcast_to(
        e_ref[pl.ds(pl.multiple_of(f * hpf, 8), 8), tok - 128 : tok][:, 127:128], (8, nst))
    e_all[c] = e_out[...]
    for k in range(1, n):
        go(e_out, e_all.at[c], s_send.at[4, k], s_recv.at[4, c], (lax.rem(c + k, n), f))

    hi, ho = rows_in // 2, rows_out // 2
    half = hi + ho
    mine = pl.ds(pl.multiple_of(core * half, 8), half)
    other = pl.ds(pl.multiple_of((1 - core) * half, 8), half)

    def place(s, which, value):
        pT[pl.ds(pl.multiple_of(s * rows_in + which * hi, 8), hi), :] = value[:hi]
        pT[pl.ds(pl.multiple_of(cin + s * rows_out + which * ho, 8), ho), :] = value[hi:]

    def to_pair(s):
        return (buf.at[s, other], core_in.at[s], p_send.at[0, s], p_recv.at[0, s], (c, fcore))

    def across(s):
        return (x_out.at[s], x_in.at[s], p_send.at[1, s], p_recv.at[1, s], (c, fx))

    def back(s):
        return (buf.at[s, mine], c_in.at[s], p_send.at[2, s], p_recv.at[2, s], (c, fcore))

    def project(s):
        left = dot1(wi_all[s], hidT[...], NN)
        right = dot1(wo_all[s], goutT[...], NN)
        buf[s, :hi] = left[:hi]
        buf[s, hi:half] = right[:ho]
        buf[s, half : half + hi] = left[hi:]
        buf[s, half + hi :] = right[ho:]
        copy(*to_pair(s)).start()

    def pair_sum(s):
        copy(*to_pair(s)).wait_recv()
        total = buf[s, mine] + core_in[s]
        buf[s, mine] = total
        x_out[s] = total.astype(bf16)
        copy(*across(s)).start()

    def full_sum(s):
        copy(*across(s)).wait_recv()
        total = buf[s, mine] + x_in[s].astype(f32)
        buf[s, mine] = total
        copy(*back(s)).start()
        place(s, core, total)

    def collect(s):
        copy(*back(s)).wait_recv()
        place(s, 1 - core, c_in[s])

    def landed(s, fwd, across_pair):
        for a, (src, dst) in enumerate(both):
            copy(dst.at[s], dst.at[s], g_send.at[2, a, s], g_recv.at[a, s], (yn, f)).wait_recv()
            if fwd is not None:
                has, to, way = fwd
                pl.when(has)(lambda: copy(
                    dst.at[s], dst.at[s], g_send.at[way, a, s], g_recv.at[a, s], (to, f)).start())
            if across_pair:
                copy(dst.at[s], dst.at[s], g_send.at[2, a, s], g_recv.at[a, s], (yn, f)).start()

    def row(k, way):
        there = z - k if way == 0 else z + k
        has = there >= 0 if way == 0 else there < outer
        q = jnp.maximum(there, 0) if way == 0 else jnp.minimum(there, outer - 1)
        fwd = (z < outer - 1, up, 0) if way == 0 else (z > 0, down, 1)
        return has, q, fwd

    events = [(None, c, None, False, False)]
    later = [(None, z * 2 + 1 - y, None, True, False)]
    for k in range(1, outer):
        for way in (0, 1):
            has, q, fwd = row(k, way)
            events.append((has, q * 2 + y, fwd, True, True))
        events.extend(later)
        later = []
        for way in (0, 1):
            has, q, fwd = row(k, way)
            later.append((has, q * 2 + 1 - y, None, True, False))
    events.extend(later)

    def under(has, fn, *args):
        if has is None:
            fn(*args)
        else:
            pl.when(has)(lambda: fn(*args))

    def take(s, fwd, wait, across_pair):
        if wait:
            landed(s, fwd, across_pair)
        project(s)

    def release(s, fwd, across_pair):
        for args in (to_pair(s), across(s), back(s)):
            copy(*args).wait_send()
        for a, (src, dst) in enumerate(both):
            def there(way, to):
                copy(dst.at[s], dst.at[s], g_send.at[way, a, s], g_recv.at[a, s],
                     (to, f)).wait_send()
            if fwd is not None:
                under(fwd[0], there, fwd[2], fwd[1])
            if across_pair:
                there(2, yn)

    total_events = len(events)
    for i in range(total_events + 5):
        if i < total_events:
            has, s, fwd, wait, across_pair = events[i]
            under(has, take, s, fwd, wait, across_pair)
        for lag, fn in ((1, pair_sum), (3, full_sum), (5, collect)):
            if 0 <= i - lag < total_events:
                under(events[i - lag][0], fn, events[i - lag][1])

    e = e_ref[...]
    einv = 1.0 / e
    eend = e[:, tok - 1 : tok]
    gate = pT[:hp, :]
    xs = pT[hp : 2 * hp, :] * einv
    bT = pT[2 * hp : 2 * hp + nst, :]
    cT = pT[2 * hp + nst : cin, :]
    xs2, b2, c2 = split(xs), split(bT), split(cT)
    tmp[...] = dot3(xs2, b2, NT) * eend
    own = pl.ds(pl.multiple_of(f * hpf, 8), hpf)
    st_out[...] = tmp[own, :]
    for k in range(n - 1, 0, -1):
        go(st_out, st_all.at[c], s_send.at[0, k], s_recv.at[0, c],
           (jnp.minimum(c + k, n - 1), f), when=c + k < n)

    upper = lax.broadcasted_iota(jnp.int32, (tok, tok), 0) <= lax.broadcasted_iota(
        jnp.int32, (tok, tok), 1)
    scores2 = split(jnp.where(upper, dot3(transposed(b2), c2, NN), 0.0))
    y_in = dot3(xs2, scores2, NN)
    sig = 1.0 / (1.0 + jnp.exp(-gate))
    silu = gate * sig

    for k in range(1, n):
        s = lax.rem(c + n - k, n)
        arrive(e_out, e_all.at[s], s_send.at[4, k], s_recv.at[4, s], (s, f))
        s = jnp.maximum(c - k, 0)
        arrive(st_out, st_all.at[s], s_send.at[0, k], s_recv.at[0, s], (s, f), when=c - k >= 0)
    state = jnp.zeros((hpf, nst), f32)
    for k in range(n - 1):
        new = e_all[k, 0:1, :] * state + st_all[k]
        state = jnp.where(k < c, new, state)
    s0_ref[own, :] = state
    for k in range(1, fs):
        go(s0_ref.at[own], s0_ref.at[own], s_send.at[1, k], s_recv.at[1, f], (c, lax.rem(f + k, fs)))
    for k in range(1, fs):
        p = lax.rem(f + fs - k, fs)
        rows = pl.ds(pl.multiple_of(p * hpf, 8), hpf)
        copy(s0_ref.at[rows], s0_ref.at[rows], s_send.at[1, k], s_recv.at[1, p], (c, p)).wait_recv()
    s02 = split(s0_ref[...])
    yT = (y_in + dot3(s02, c2, NN)) * e

    gain = jnp.broadcast_to(gain_ref[...].reshape(1, hp), (8, hp)).T[:, 0:1]
    gated = yT * silu
    r = lax.rsqrt(jnp.mean(gated * gated, axis=0, keepdims=True) + EPS)
    normed = (gated * r * gain).astype(bf16)
    u = pT[cin:, :] * gain
    dgated = r * u - gated * (r * r * r * jnp.mean(u * gated, axis=0, keepdims=True))
    dys2 = split(dgated * silu * e)
    tmp[...] = dot3(dys2, c2, NT)
    ad_out[...] = tmp[own, :].astype(bf16)
    for k in range(n - 1, 0, -1):
        go(ad_out, ad_all.at[c], s_send.at[2, k], s_recv.at[2, c],
           (jnp.maximum(c - k, 0), f), when=c - k >= 0)
    gp[:hp, :] = (dgated * yT * (sig * (1.0 + gate * (1.0 - sig)))).astype(bf16)

    ro[...] = dot1(normed, gout_ref[...], NN)
    for q in range(outer):
        at = pl.ds(pl.multiple_of((q * 2 + 1 - y) * rows_out, 8), rows_out)
        ob1[q] = ro[at, :].astype(bf16)
    go(ob1, ob1r, o_send.at[0], o_recv.at[0], (yn, f))

    dscores = jnp.where(upper, dot1(xs2[0].T, dys2[0], NN), 0.0).astype(bf16)
    gp[2 * hp + nst :, :] = (dot1(b2[0], dscores, NN) + dot3(transposed(s02), dys2, NN)).astype(bf16)
    db = dot1(c2[0], dscores, NT)
    dxs = dot1(dys2[0], scores2[0], NT)

    for k in range(1, n):
        s = jnp.minimum(c + k, n - 1)
        arrive(ad_out, ad_all.at[s], s_send.at[2, k], s_recv.at[2, s], (s, f), when=c + k < n)
    adj = jnp.zeros((hpf, nst), f32)
    for k in range(n - 1, 0, -1):
        new = e_all[k, 0:1, :] * adj + ad_all[k].astype(f32)
        adj = jnp.where(k > c, new, adj)
    g_ref[own, :] = adj
    for k in range(1, fs):
        go(g_ref.at[own], g_ref.at[own], s_send.at[3, k], s_recv.at[3, f], (c, lax.rem(f + k, fs)))
    for k in range(1, fs):
        p = lax.rem(f + fs - k, fs)
        rows = pl.ds(pl.multiple_of(p * hpf, 8), hpf)
        copy(g_ref.at[rows], g_ref.at[rows], s_send.at[3, k], s_recv.at[3, p], (c, p)).wait_recv()
    g2 = split(g_ref[...] * eend)
    gp[hp : 2 * hp, :] = ((dxs + dot3(g2, b2, NN)) * einv).astype(bf16)
    gp[2 * hp : 2 * hp + nst, :] = (db + dot3(transposed(g2), xs2, NN)).astype(bf16)

    copy(ob1, ob1r, o_send.at[0], o_recv.at[0], (yn, f)).wait_recv()
    for q in range(outer):
        at = pl.ds(pl.multiple_of((q * 2 + y) * rows_out, 8), rows_out)
        total = ro[at, :] + ob1r[q].astype(f32)
        ro[at, :] = total
        ob2[q] = total.astype(bf16)

    for k in range(1, outer):
        q = lax.rem(z + k, outer)
        go(ob2.at[q], ob2r.at[z], o_send.at[k], o_recv.at[1 + z], (q * 2 + y, f))

    def rows_of(s):
        return pl.ds(pl.multiple_of(s * rows_in, 16), rows_in)

    far = order[::-1] + [0]
    for i, k in enumerate(far):
        q = lax.rem(z + k, outer)
        ib1[i] = dot1(gp[rows_of(q * 2 + 1 - y), :], hid_ref[...], NN).astype(bf16)
        go(ib1.at[i], ib1r.at[i], i_send.at[0, i], i_recv.at[0, i], (yn, f))
    for i, k in enumerate(far):
        q = lax.rem(z + k, outer)
        part = dot1(gp[rows_of(q * 2 + y), :], hid_ref[...], NN)
        copy(ib1.at[i], ib1r.at[i], i_send.at[0, i], i_recv.at[0, i], (yn, f)).wait_recv()
        part = part + ib1r[i].astype(f32)
        if k:
            ib2[i] = part.astype(bf16)
            go(ib2.at[i], ib2r.at[z], i_send.at[1, i], i_recv.at[1, z], (q * 2 + y, f))
        else:
            ri[...] = part

    acc = ro[pl.ds(pl.multiple_of(c * rows_out, 8), rows_out), :]
    for k in range(1, outer):
        q = lax.rem(z + k, outer)
        copy(ob2.at[q], ob2r.at[q], o_send.at[k], o_recv.at[1 + q], (q * 2 + y, f)).wait_recv()
        acc = acc + ob2r[q].astype(f32)
    acc = acc * (1.0 / root_tokens)
    ro[:rows_out, :] = acc
    nout_out[...] = jnp.sum(acc * acc, axis=0, keepdims=True).reshape(8, d // 8)
    for k in range(1, n):
        go(nout_out, nout_all.at[c], n_send.at[0, k], n_recv.at[0, c], (lax.rem(c + k, n), f))
    nout_all[c] = nout_out[...]

    gpt = gp[...].T
    wi = wi_all[...].reshape(cin, d)
    gh_ref[...] = dot1(gpt, wi, NN).astype(bf16)
    put_gh = pltpu.make_async_copy(gh_ref, gh_any, l_sem.at[6])
    put_gh.start()

    weight = jnp.zeros((1, d), f32)
    for s in range(n):
        w = wo_all[s].astype(f32)
        weight = weight + jnp.sum(w * w, axis=0, keepdims=True)
    w = wi_all[c].astype(f32)
    weight_in = jnp.sum(w * w, axis=1, keepdims=True)

    acc = ri[...]
    for k in range(1, outer):
        q = lax.rem(z + k, outer)
        copy(ib2.at[0], ib2r.at[q], i_send.at[1, 0], i_recv.at[1, q], (q * 2 + y, f)).wait_recv()
        acc = acc + ib2r[q].astype(f32)
    acc = acc * (1.0 / root_tokens)
    ri[...] = acc
    at = lax.broadcasted_iota(jnp.int32, (rows_in, 128), 1)
    nin_out[...] = jnp.where(at < 64, jnp.sum(acc * acc, axis=1, keepdims=True), weight_in)
    for k in range(1, fs):
        go(nin_out, nin_all.at[f], n_send.at[1, k], n_recv.at[1, f], (c, lax.rem(f + k, fs)))
    nin_all[f] = nin_out[...]

    grad_square = nout_all[c]
    for k in range(1, n):
        s = lax.rem(c + n - k, n)
        copy(nout_out, nout_all.at[s], n_send.at[0, k], n_recv.at[0, s], (s, f)).wait_recv()
        grad_square = grad_square + nout_all[s]
    grad_square = grad_square.reshape(1, d)
    factor = jnp.minimum(1.0, clip_output * jnp.maximum(jnp.sqrt(weight), 0.001)
                         / jnp.maximum(jnp.sqrt(grad_square), 1e-06))
    gwo_ref[...] = ro[:rows_out, :] * factor
    put_gwo = pltpu.make_async_copy(gwo_ref, gwo_any, l_sem.at[7])
    put_gwo.start()

    square = nin_all[f]
    for k in range(1, fs):
        p = lax.rem(f + fs - k, fs)
        copy(nin_out, nin_all.at[p], n_send.at[1, k], n_recv.at[1, p], (c, p)).wait_recv()
        square = square + nin_all[p]
    root = jnp.sqrt(square)
    factor = jnp.minimum(1.0, clip_input * jnp.maximum(root[:, 64:65], 0.001)
                         / jnp.maximum(root[:, 0:1], 1e-06))
    gwi_ref[...] = ri[...] * factor
    put_gwi = pltpu.make_async_copy(gwi_ref, gwi_any, l_sem.at[8])
    put_gwi.start()
    for has, args in sent:
        under(has, lambda args: copy(*args).wait_send(), args)
    for has, s, fwd, wait, across_pair in events:
        under(has, release, s, fwd, across_pair)
    put_gh.wait()
    put_gwo.wait()
    put_gwi.wait()


def one_kernel(n, fs, hidden, w_in, decay, norm_gain, w_out, grad_out):
    tok, d = hidden.shape
    rows_in, rows_out = w_in.shape[0], w_out.shape[0]
    cin, hp = rows_in * n, rows_out * n
    nst = (cin - 2 * hp) // 2
    hpf, outer = hp // fs, n // 2
    half = (rows_in + rows_out) // 2
    V = pltpu.VMEM
    dma = pltpu.SemaphoreType.DMA
    scratch = [
        V((d, tok), bf16), V((d, tok), bf16), V((n, rows_in, d), bf16), V((n, rows_out, d), bf16),
        V((cin + hp, tok), f32), V((n, 2 * half, tok), f32), V((n, half, tok), f32),
        V((n, half, tok), bf16), V((n, half, tok), bf16), V((n, half, tok), f32),
        V((8, nst), f32), V((n, 8, nst), f32),
        V((hp, tok), f32), V((hpf, nst), f32), V((n, hpf, nst), f32), V((hp, nst), f32),
        V((hpf, nst), bf16), V((n, hpf, nst), bf16), V((hp, nst), f32),
        V((hp, d), f32), V((outer, rows_out, d), bf16), V((outer, rows_out, d), bf16),
        V((outer, rows_out, d), bf16), V((outer, rows_out, d), bf16),
        V((cin, tok), bf16), V((rows_in, d), f32),
        V((outer, rows_in, d), bf16), V((outer, rows_in, d), bf16),
        V((outer, rows_in, d), bf16), V((outer, rows_in, d), bf16),
        V((rows_in, 128), f32), V((fs, rows_in, 128), f32), V((8, d // 8), f32), V((n, 8, d // 8), f32),
        dma((3, 2, n)), dma((2, n)), dma((3, n)), dma((3, n)), dma((5, n)), dma((5, n)),
        dma((1 + outer,)), dma((1 + outer,)), dma((2, outer)), dma((2, outer)),
        dma((2, n)), dma((2, n)), V((hp, nst), f32),
        V((tok, d), bf16), V((tok, d), bf16), V(decay.shape, f32), V((hp,), f32),
        V((tok, d), bf16), V((rows_in, d), f32), V((rows_out, d), f32), dma((9,)),
    ]
    return pl.pallas_call(
        functools.partial(fused, n, fs, math.sqrt(tok * n), math.sqrt(d * fs)),
        out_shape=(
            V((tok, d), bf16),
            V((rows_in, d), f32),
            V((rows_out, d), f32),
        ),
        in_specs=[pl.BlockSpec(memory_space=pl.ANY)] * 6,
        out_specs=(pl.BlockSpec(memory_space=pl.ANY),) * 3,
        scratch_shapes=scratch,
        compiler_params=pltpu.CompilerParams(
            collective_id=0, has_side_effects=True, vmem_limit_bytes=60 * 1024 * 1024),
    )(hidden, w_in, decay, norm_gain, w_out, grad_out)


def solution(mesh):
    n, fs = mesh.shape["ctx"], mesh.shape["fsdp"]

    def body(hidden, w_in, decay, norm_gain, w_out, grad_out):
        whole_tiles = w_in.shape[0] % 16 == 0 and w_out.shape[0] % 16 == 0
        if whole_tiles and fs == decay.shape[0] and fs % 2 == 0 and n % 2 == 0 and n >= 4:
            return one_kernel(n, fs, hidden, w_in, decay, norm_gain, w_out, grad_out)
        return local(hidden, w_in, decay, norm_gain, w_out, grad_out)

    return jax.shard_map(
        body,
        mesh=mesh,
        in_specs=(
            P("ctx", "fsdp"),
            P("ctx", "fsdp"),
            P(None, "ctx"),
            P(),
            P("ctx", "fsdp"),
            P("ctx", "fsdp"),
        ),
        out_specs=(P("ctx", "fsdp"), P("ctx", "fsdp"), P("ctx", "fsdp")),
        check_vma=False,
    )
```

```python
import functools
import math

import jax
import jax.numpy as jnp
from jax import lax
from jax.experimental import pallas as pl
from jax.experimental.pallas import tpu as pltpu
from jax.sharding import PartitionSpec as P

D = 4096
H = 4
P_SIZE = 64
N = 128
HP = 256


highest = lax.Precision.HIGHEST
clip_output = 10.0


def prefix(x, axis, combine, identity):
    count, index = (lax.axis_size(axis), lax.axis_index(axis))
    everything = jax.tree.map(lambda part: lax.all_gather(part, axis), x)
    start = jax.tree.map(
        lambda part, zero: jnp.broadcast_to(jnp.asarray(zero, part.dtype), part.shape), x, identity
    )

    def step(k, before):
        reached = k < index
        new = combine(before, jax.tree.map(lambda part: part[k], everything))
        return jax.tree.map(lambda a, b: jnp.where(reached, a, b), new, before)

    return lax.fori_loop(0, count, step, start)


def entering(x, axis, join, neutral):
    count = lax.axis_size(axis)
    place = lax.axis_index(axis)
    ahead = count - 1 - place
    gathered = jax.tree.map(
        lambda a, kind: lax.all_gather(a.astype(kind), axis),
        x,
        jax.tree.map(lambda a: jnp.bfloat16 if a.dtype == jnp.float32 else a.dtype, x),
    )
    state = jax.tree.map(lambda a, e: jnp.zeros_like(a) + jnp.asarray(e, a.dtype), x, neutral)

    def one(step, state):
        source = count - 1 - step
        return join(
            state,
            jax.tree.map(
                lambda a, own: lax.dynamic_index_in_dim(a, source, 0, False).astype(own.dtype),
                gathered,
                x,
            ),
        )

    return lax.fori_loop(0, ahead, one, state)


def split_columns(projection):
    return (
        projection[:, :HP],
        projection[:, HP : 2 * HP],
        projection[:, 2 * HP : 2 * HP + N],
        projection[:, 2 * HP + N :],
    )


def intra_block(x_part, b_part, c_part, log_decay):
    length = x_part.shape[0]
    cum_decay = jnp.cumsum(log_decay, axis=1)
    x_heads = x_part.reshape(length, H, P_SIZE)
    causal = jnp.arange(length)[:, None] >= jnp.arange(length)[None, :]
    gaps = jnp.where(causal[None], cum_decay[:, :, None] - cum_decay[:, None, :], 0.0)
    weights = jnp.where(causal[None], jnp.exp(gaps), 0.0)
    scores = jnp.dot(c_part, b_part.T, precision=highest)
    mixed = weights * scores[None]
    y_intra = jnp.einsum("hts,shp->thp", mixed, x_heads, precision=highest).reshape(
        length, H * P_SIZE
    )
    tail = jnp.exp(cum_decay[:, -1:] - cum_decay)
    weighted = x_heads * tail.T[:, :, None]
    state_part = jnp.einsum("shp,sn->hpn", weighted, b_part, precision=highest)
    return (y_intra, state_part, cum_decay)


def finish_block(gate_part, y_intra, c_part, start_state, cum_decay, norm_gain):
    length = c_part.shape[0]
    carried = jnp.einsum("hpn,tn->thp", start_state, c_part, precision=highest)
    carried = carried * jnp.exp(cum_decay).T[:, :, None]
    y_full = y_intra + carried.reshape(length, H * P_SIZE)
    gated = y_full * jax.nn.silu(gate_part)
    factor = lax.rsqrt(jnp.mean(gated * gated, axis=-1, keepdims=True) + 1e-05)
    return gated * factor * norm_gain


def carry_states(earlier, later):
    return (earlier[0] * later[0], later[0] * earlier[1] + later[1])


def carry_adjoint(earlier, later):
    return (earlier[0] * later[0], later[1] + later[0] * earlier[1])


def local(hidden, w_in, decay, norm_gain, w_out, grad_out):
    clip_input = math.sqrt(D)
    tok_rows = hidden.shape[0]
    root_tokens = math.sqrt(tok_rows * lax.axis_size("ctx"))
    contract_last = (((1,), (1,)), ((), ()))
    contract_first = (((0,), (0,)), ((), ()))
    partial_proj = lax.dot_general(
        hidden,
        lax.all_gather(w_in, "ctx", axis=0, tiled=True),
        contract_last,
        preferred_element_type=jnp.float32,
    )
    slab_out = lax.all_gather(w_out, "ctx", axis=0, tiled=True)
    partial_grad = lax.dot_general(
        grad_out, slab_out, contract_last, preferred_element_type=jnp.float32
    )
    projection, grad_normed = lax.psum((partial_proj, partial_grad), "fsdp")
    log_decay = jnp.log(decay)
    gate_part, x_part, b_part, c_part = split_columns(projection)

    def intra_only(x_value, b_value, c_value):
        return intra_block(x_value, b_value, c_value, log_decay)

    (y_intra, state_part, cum_decay), intra_pull = jax.vjp(intra_only, x_part, b_part, c_part)
    decay_total = jnp.exp(cum_decay[:, -1])[:, None, None]
    identity = (jnp.ones_like(decay_total), jnp.zeros_like(state_part))
    _, start_state = prefix((decay_total, state_part), "ctx", carry_states, identity)

    def finish_only(gate_value, intra_value, c_value, state_value):
        return finish_block(gate_value, intra_value, c_value, state_value, cum_decay, norm_gain)

    normed, finish_pull = jax.vjp(finish_only, gate_part, y_intra, c_part, start_state)
    grad_gate, grad_intra, grad_c_late, grad_start = finish_pull(grad_normed)
    _, grad_end = entering((decay_total, grad_start), "ctx", carry_adjoint, identity)
    grad_x, grad_b, grad_c_early = intra_pull((grad_intra, grad_end, jnp.zeros_like(cum_decay)))
    grad_projection = jnp.concatenate(
        [grad_gate, grad_x, grad_b, grad_c_early + grad_c_late], axis=1
    ).astype(jnp.bfloat16)
    columns = grad_projection
    grad_hidden = jnp.dot(
        columns, lax.all_gather(w_in, "ctx", axis=0, tiled=True), preferred_element_type=jnp.float32
    )
    columns = grad_projection
    raw_in = (
        lax.psum_scatter(
            lax.dot_general(columns, hidden, contract_first, preferred_element_type=jnp.float32),
            "ctx",
            scatter_dimension=0,
            tiled=True,
        )
        / root_tokens
    )
    weight_square = jnp.sum(jnp.square(w_in.astype(jnp.float32)), axis=1)
    weight_in, grad_in = lax.psum((weight_square, jnp.sum(raw_in * raw_in, axis=1)), "fsdp")
    factor_in = jnp.minimum(
        1.0,
        clip_input
        * jnp.maximum(jnp.sqrt(weight_in), 0.001)
        / jnp.maximum(jnp.sqrt(grad_in), 1e-06),
    )
    normed_rounded = normed.astype(jnp.bfloat16)
    weight_out = jnp.sqrt(jnp.sum(jnp.square(slab_out.astype(jnp.float32)), axis=0))
    raw_out = (
        lax.psum_scatter(
            lax.dot_general(
                normed_rounded, grad_out, contract_first, preferred_element_type=jnp.float32
            ),
            "ctx",
            scatter_dimension=0,
            tiled=True,
        )
        / root_tokens
    )
    grad_square = lax.psum(jnp.sum(raw_out * raw_out, axis=0), "ctx")
    factor_out = jnp.minimum(
        1.0,
        clip_output * jnp.maximum(weight_out, 0.001) / jnp.maximum(jnp.sqrt(grad_square), 1e-06),
    )
    return (
        grad_hidden.astype(jnp.bfloat16),
        raw_in * factor_in[:, None],
        raw_out * factor_out[None, :],
    )


NN = (((1,), (0,)), ((), ()))
NT = (((1,), (1,)), ((), ()))
TN = (((0,), (0,)), ((), ()))
MESH = pl.DeviceIdType.MESH
f32 = jnp.float32
bf16 = jnp.bfloat16
EPS = 1e-05


def split(a):
    hi = a.astype(bf16)
    return hi, (a - hi.astype(f32)).astype(bf16)


def dot1(a, b, dims):
    return lax.dot_general(a, b, dims, preferred_element_type=f32)


def dot3(a, b, dims):
    return dot1(a[0], b[0], dims) + (dot1(a[0], b[1], dims) + dot1(a[1], b[0], dims))


def transposed(pair):
    return pair[0].T, pair[1].T


def early_and_late(n, rows, hp, nst):
    g = math.gcd(rows, math.gcd(hp, nst))
    early, late = [], []
    for y in (0, 1):
        first, last = [], []
        for q in range(n // 2):
            for j in range(rows // g):
                row = (q * 2 + y) * rows + j * g
                soon = row + g <= hp or row >= 2 * hp + nst
                (first if soon else last).append((row, q, j))
        early.append(first)
        late.append(last)
    return g, early, late


def fits(n, w_in, w_out):
    rows, hp = w_in.shape[0], w_out.shape[0] * n
    nst = (rows * n - 2 * hp) // 2
    g, early, late = early_and_late(n, rows, hp, nst)
    same = len(early[0]) == len(early[1]) and len(early[0]) >= 2
    return g % 16 == 0 and same and w_in.shape[1] % 1024 == 0


def fused(
    n, fs, root_tokens, clip_input,
    hid_any, win_ref, dec_any, gain_any, wout_ref, gout_any,
    gh_any, gwi_any, gwo_any,
    hidT, goutT, wi_all, wo_all, pT,
    bi, ai_in, xi_out, xi_in, ci_in, bo, ao_in, xo_out, xo_in, co_in,
    e_out, e_all, e_ref, st_out, st_all, s0_ref, ad_out, ad_all, g_ref,
    ro, ob1, ob1r, ob2, ob2r, gp, rin, ri, ib1, ib1r, ib2, ib2r,
    nin_out, nin_all, nout_out, nout_all,
    g_send, g_recv, pi_send, pi_recv, po_send, po_recv, s_send, s_recv, t_send, t_recv,
    o_send, o_recv, i_send, iy_recv, iz_recv, n_send, n_recv, tmp,
    hid_ref, gout_ref, dec_ref, gain_ref, gh_ref, gwi_ref, gwo_ref, l_sem,
):
    c = lax.axis_index("ctx")
    f = lax.axis_index("fsdp")
    outer = n // 2
    z, y = c // 2, lax.rem(c, 2)
    yn = c + 1 - 2 * y
    core = lax.rem(f, 2)
    fcore = f + 1 - 2 * core
    fx = lax.rem(f + fs // 2, fs)
    rows_in, d = win_ref.shape
    rows_out = wout_ref.shape[0]
    tok = hid_any.shape[0]
    cin, hp = rows_in * n, rows_out * n
    nst = (cin - 2 * hp) // 2
    hpf = hp // fs
    first = hp // rows_in
    g, early, late = early_and_late(n, rows_in, hp, nst)

    def copy(src, dst, ssem, rsem, dev):
        return pltpu.make_async_remote_copy(
            src_ref=src, dst_ref=dst, send_sem=ssem, recv_sem=rsem,
            device_id=dev, device_id_type=MESH)

    ends = []

    def under(has, fn, *args):
        if has is None:
            fn(*args)
        else:
            pl.when(has)(lambda: fn(*args))

    def start(*args, when=None):
        under(when, lambda: copy(*args).start())

    def go(*args, when=None):
        start(*args, when=when)
        ends.append((when, args))

    def total(src, dst, sem, rsem, when=None):
        ends.append((when, (src, dst, sem, rsem, (yn, f))))

    local = [
        pltpu.make_async_copy(src, dst, l_sem.at[i])
        for i, (src, dst) in enumerate((
            (hid_any, hid_ref), (win_ref, wi_all.at[c]), (gout_any, gout_ref),
            (wout_ref, wo_all.at[c]), (dec_any, dec_ref), (gain_any, gain_ref)))
    ]
    for each in local:
        each.start()

    barrier = pltpu.get_barrier_semaphore()
    for k in range(1, n):
        pl.semaphore_signal(barrier, inc=1, device_id=(lax.rem(c + k, n), f), device_id_type=MESH)
    for k in range(1, fs):
        pl.semaphore_signal(barrier, inc=1, device_id=(c, lax.rem(f + k, fs)), device_id_type=MESH)
    pl.semaphore_wait(barrier, n + fs - 2)

    both = ((win_ref, wi_all), (wout_ref, wo_all))
    up = jnp.minimum(z + 1, outer - 1) * 2 + y
    down = jnp.maximum(z - 1, 0) * 2 + y

    pieces = (rows_in // g, 1)

    def part(ref, a, s, j):
        return ref.at[s] if a else ref.at[s, pl.ds(j * g, g)]

    def own(a):
        src, dst = both[a]
        for j in range(pieces[a]):
            to = part(dst, a, c, j)
            at = src if a else src.at[pl.ds(j * g, g)]
            sem = g_recv.at[a, c, j]
            start(at, to, g_send.at[0, a], sem, (up, f), when=z < outer - 1)
            start(at, to, g_send.at[1, a], sem, (down, f), when=z > 0)
            start(at, to, g_send.at[2, a], sem, (yn, f))

    def landed_part(a, s, j):
        at = part(both[a][1], a, s, j)
        copy(at, at, g_send.at[2, a], g_recv.at[a, s, j], (yn, f)).wait_recv()

    def landed(a, s):
        for j in range(pieces[a]):
            landed_part(a, s, j)

    def relay(a, s, fwd, j):
        at = part(both[a][1], a, s, j)
        has, to, way = fwd
        landed_part(a, s, j)
        start(at, at, g_send.at[way, a], g_recv.at[a, s, j], (to, f), when=has)
        start(at, at, g_send.at[2, a], g_recv.at[a, s, j], (yn, f))

    own(0)
    for each in local[:2]:
        each.wait()
    hidT[...] = hid_ref[...].T

    hi = rows_in // 2
    mine = pl.ds(pl.multiple_of(core * hi, 8), hi)
    other = pl.ds(pl.multiple_of((1 - core) * hi, 8), hi)
    mine_o = pl.ds(pl.multiple_of(core * rows_out, 8), rows_out)
    other_o = pl.ds(pl.multiple_of((1 - core) * rows_out, 8), rows_out)

    class Chain:
        def __init__(self, part, pair_in, x_out, x_in, back_in, send, recv, mine, other, base):
            self.part, self.pair_in, self.x_out, self.x_in = part, pair_in, x_out, x_in
            self.back_in, self.send, self.recv, self.base = back_in, send, recv, base
            self.mine, self.other, self.half = mine, other, pair_in.shape[1]

        def to_pair(self, s):
            return copy(self.part.at[s, self.other], self.pair_in.at[s], self.send.at[0],
                        self.recv.at[0, s], (c, fcore))

        def across(self, s):
            return copy(self.x_out.at[s], self.x_in.at[s], self.send.at[1],
                        self.recv.at[1, s], (c, fx))

        def back(self, s):
            return copy(self.part.at[s, self.mine], self.back_in.at[s], self.send.at[2],
                        self.recv.at[2, s], (c, fcore))

        def place(self, s, which, value):
            at = self.base + s * (2 * self.half) + which * self.half
            pT[pl.ds(pl.multiple_of(at, 8), self.half), :] = value

        def take(self, s, value):
            self.part[s] = value
            self.to_pair(s).start()

        def pair_sum(self, s):
            self.to_pair(s).wait_recv()
            value = self.part[s, self.mine] + self.pair_in[s]
            self.part[s, self.mine] = value
            self.x_out[s] = value.astype(bf16)
            self.across(s).start()

        def full_sum(self, s):
            self.across(s).wait_recv()
            value = self.part[s, self.mine] + self.x_in[s].astype(f32)
            self.part[s, self.mine] = value
            self.back(s).start()
            self.place(s, core, value)

        def collect(self, s):
            self.back(s).wait_recv()
            self.place(s, 1 - core, self.back_in[s])

        def finish(self):
            total(self.pair_in, self.pair_in, self.send.at[0], self.recv.at[0, 0])
            total(self.x_out, self.x_in, self.send.at[1], self.recv.at[1, 0])
            total(self.back_in, self.back_in, self.send.at[2], self.recv.at[2, 0])

    ins = Chain(bi, ai_in, xi_out, xi_in, ci_in, pi_send, pi_recv, mine, other, 0)
    outs = Chain(bo, ao_in, xo_out, xo_in, co_in, po_send, po_recv, mine_o, other_o, cin)

    def both_true(a, b):
        return b if a is None else jnp.logical_and(a, b)

    def row(k, way):
        there = z - k if way == 0 else z + k
        has = there >= 0 if way == 0 else there < outer
        q = jnp.maximum(there, 0) if way == 0 else jnp.minimum(there, outer - 1)
        fwd = (z < outer - 1, up, 0) if way == 0 else (z > 0, down, 1)
        return has, q, fwd

    def take_in(s):
        ins.take(s, dot1(wi_all[s], hidT[...], NN))

    def soon(has, s):
        return both_true(has, s >= first)

    def behind(k):
        if k == 0:
            own(1)
            return
        for j in range(pieces[0]):
            for way in (0, 1):
                has, q, fwd = row(k, way)
                s = q * 2 + y
                under(both_true(has, s < first), relay, 0, s, fwd, j)
        for way in (0, 1):
            has, q, fwd = row(k, way)
            under(has, relay, 1, q * 2 + y, fwd, 0)

    def ahead(k):
        for j in range(pieces[0]):
            for way in (0, 1):
                has, q, fwd = row(k, way)
                s = q * 2 + y
                under(soon(has, s), relay, 0, s, fwd, j)

    def crossed(s):
        landed(0, s)
        take_in(s)

    def run(steps, lags):
        done = []

        def trail(i):
            for lag, name in zip(lags, ("pair_sum", "full_sum", "collect")):
                if 0 <= i - lag < len(done):
                    has, s, chain = done[i - lag]
                    under(has, getattr(chain, name), s)

        for has, fn, arg, chain in steps:
            under(has, fn, arg)
            if chain is not None:
                done.append((has, arg, chain))
                trail(len(done) - 1)

        def rest():
            for i in range(len(done), len(done) + lags[-1]):
                trail(i)

        return rest

    steps = [(soon(None, c), take_in, c, ins), (None, ahead, 1, None)]
    later = [(soon(None, yn), crossed, yn, ins)]
    for k in range(1, outer):
        if k > 1:
            steps.append((None, ahead, k, None))
        for way in (0, 1):
            has, q, _ = row(k, way)
            s = q * 2 + y
            steps.append((soon(has, s), take_in, s, ins))
        steps.extend(later)
        steps.append((None, behind, k - 1, None))
        later = []
        for way in (0, 1):
            has, q, _ = row(k, way)
            s = q * 2 + 1 - y
            later.append((soon(has, s), crossed, s, ins))
    steps.extend(later)

    def decays():
        decay = dec_ref[...]
        lane = lax.broadcasted_iota(jnp.int32, decay.shape, 1)
        shift = 1
        while shift < tok:
            decay = decay * jnp.where(lane >= shift, pltpu.roll(decay, shift, 1), 1.0)
            shift *= 2
        heads = decay.shape[0]
        for h in range(heads):
            e_ref[h * (hp // heads) : (h + 1) * (hp // heads), :] = jnp.broadcast_to(
                decay[h : h + 1], (hp // heads, tok))
        e_out[...] = jnp.broadcast_to(
            e_ref[pl.ds(pl.multiple_of(f * hpf, 8), 8), tok - 128 : tok][:, 127:128], (8, nst))
        e_all[c] = e_out[...]
        for k in range(1, n):
            start(e_out, e_all.at[c], t_send.at[0], t_recv.at[0, c], (lax.rem(c + k, n), f))
        total(e_all.at[pl.ds(0, n - 1)], e_all.at[pl.ds(0, n - 1)], t_send.at[0], t_recv.at[0, 0])

    for each in local[2:]:
        each.wait()
    goutT[...] = gout_ref[...].T
    decays()
    run(steps, (2, 5, 8))()

    e = e_ref[...]
    einv = 1.0 / e
    eend = e[:, tok - 1 : tok]
    xs = pT[hp : 2 * hp, :] * einv
    bT = pT[2 * hp : 2 * hp + nst, :]
    cT = pT[2 * hp + nst : cin, :]
    xs2, b2, c2 = split(xs), split(bT), split(cT)
    tmp[...] = dot3(xs2, b2, NT) * eend
    own_rows = pl.ds(pl.multiple_of(f * hpf, 8), hpf)
    st_out[...] = tmp[own_rows, :]
    for k in range(n - 1, 0, -1):
        go(st_out, st_all.at[c], s_send.at[0, k], s_recv.at[0, c],
           (jnp.minimum(c + k, n - 1), f), when=c + k < n)

    upper = lax.broadcasted_iota(jnp.int32, (tok, tok), 0) <= lax.broadcasted_iota(
        jnp.int32, (tok, tok), 1)
    scores2 = split(jnp.where(upper, dot3(transposed(b2), c2, NN), 0.0))
    y_in = dot3(xs2, scores2, NN)
    behind(outer - 1)

    def take_gate(s):
        under(lax.rem(s + y, 2) != 0, landed, 0, s)
        take_in(s)

    def take_out(q):
        landed(1, q * 2 + 1 - y)
        at = pl.ds(pl.multiple_of(q * 2, 2), 2)
        outs.take(q, dot1(wo_all[at].reshape(2 * rows_out, d), goutT[...], NN))

    more = [(None, take_out, z, outs)]
    for k in range(1, outer):
        if k == outer - 1:
            more.extend((None, take_gate, s, ins) for s in range(first))
        for way in (0, 1):
            has, q, _ = row(k, way)
            more.append((has, take_out, q, outs))
    rest = run(more, (2, 4, 6))

    for k in range(1, n):
        s = lax.rem(c + n - k, n)
        copy(e_out, e_all.at[s], t_send.at[0], t_recv.at[0, s], (s, f)).wait_recv()
        s = jnp.maximum(c - k, 0)
        pl.when(c - k >= 0)(lambda s=s, k=k: copy(
            st_out, st_all.at[s], s_send.at[0, k], s_recv.at[0, s], (s, f)).wait_recv())
    state = jnp.zeros((hpf, nst), f32)
    for k in range(n - 1):
        new = e_all[k, 0:1, :] * state + st_all[k]
        state = jnp.where(k < c, new, state)
    s0_ref[own_rows, :] = state

    def share(ref, i):
        for k in range(1, fs):
            start(ref.at[own_rows], ref.at[own_rows], t_send.at[i], t_recv.at[i, f],
                  (c, lax.rem(f + k, fs)))
        total(st_all.at[pl.ds(0, fs - 1)], st_all.at[pl.ds(0, fs - 1)], t_send.at[i],
              t_recv.at[i, 0])

    def shared(ref, i):
        for k in range(1, fs):
            p = lax.rem(f + fs - k, fs)
            rows = pl.ds(pl.multiple_of(p * hpf, 8), hpf)
            copy(ref.at[rows], ref.at[rows], t_send.at[i], t_recv.at[i, p], (c, p)).wait_recv()

    share(s0_ref, 1)
    rest()
    gate = pT[:hp, :]
    sig = 1.0 / (1.0 + jnp.exp(-gate))
    silu = gate * sig

    shared(s0_ref, 1)
    s02 = split(s0_ref[...])
    yT = (y_in + dot3(s02, c2, NN)) * e

    gain = jnp.broadcast_to(gain_ref[...].reshape(1, hp), (8, hp)).T[:, 0:1]
    gated = yT * silu
    r = lax.rsqrt(jnp.mean(gated * gated, axis=0, keepdims=True) + EPS)
    normed = (gated * r * gain).astype(bf16)
    u = pT[cin:, :] * gain
    dgated = r * u - gated * (r * r * r * jnp.mean(u * gated, axis=0, keepdims=True))
    dys2 = split(dgated * silu * e)
    tmp[...] = dot3(dys2, c2, NT)
    ad_out[...] = tmp[own_rows, :].astype(bf16)
    for k in range(n - 1, 0, -1):
        go(ad_out, ad_all.at[c], s_send.at[1, k], s_recv.at[1, c],
           (jnp.maximum(c - k, 0), f), when=c - k >= 0)

    ro[...] = dot1(normed, gout_ref[...], NN)
    for q in range(outer):
        at = pl.ds(pl.multiple_of((q * 2 + 1 - y) * rows_out, 8), rows_out)
        ob1[q] = ro[at, :].astype(bf16)
    go(ob1, ob1r, o_send.at[0], o_recv.at[0], (yn, f))

    blocks = [early[0] + late[0], early[1] + late[1]]
    n_early, n_blocks = len(early[0]), len(blocks[0])

    def pick(i, part, side):
        a, b = blocks[0][i][part], blocks[1][i][part]
        return a + side * (b - a)

    def to_partner(lo, hi):
        for i in range(lo, hi):
            at = pl.ds(pl.multiple_of(pick(i, 0, 1 - y), 8), g)
            ib1[i] = rin[at, :].astype(bf16)
            start(ib1.at[i], ib1r.at[i], i_send.at[0], iy_recv.at[i], (yn, f))

    def merge(lo, hi):
        for i in range(lo, hi):
            copy(ib1.at[i], ib1r.at[i], i_send.at[0], iy_recv.at[i], (yn, f)).wait_recv()
            at = pl.ds(pl.multiple_of(pick(i, 0, y), 8), g)
            value = rin[at, :] + ib1r[i].astype(f32)
            q, j = pick(i, 1, y), pick(i, 2, y)

            def keep():
                ri[pl.ds(pl.multiple_of(j * g, 8), g), :] = value

            def send():
                ib2[i] = value.astype(bf16)
                copy(ib2.at[i], ib2r.at[z, j], i_send.at[1], iz_recv.at[0], (q * 2 + y, f)).start()

            pl.when(q == z)(keep)
            pl.when(q != z)(send)

    dscores = jnp.where(upper, dot1(xs2[0].T, dys2[0], NN), 0.0).astype(bf16)
    gp[:hp, :] = (dgated * yT * (sig * (1.0 + gate * (1.0 - sig)))).astype(bf16)
    rin[:hp, :] = dot1(gp[:hp, :], hid_ref[...], NN)
    gp[2 * hp + nst :, :] = (dot1(b2[0], dscores, NN) + dot3(transposed(s02), dys2, NN)).astype(bf16)
    rin[2 * hp + nst :, :] = dot1(gp[2 * hp + nst :, :], hid_ref[...], NN)
    to_partner(0, n_early)
    db = dot1(c2[0], dscores, NT)
    dxs = dot1(dys2[0], scores2[0], NT)

    for k in range(1, n):
        s = jnp.minimum(c + k, n - 1)
        pl.when(c + k < n)(lambda s=s, k=k: copy(
            ad_out, ad_all.at[s], s_send.at[1, k], s_recv.at[1, s], (s, f)).wait_recv())
    adj = jnp.zeros((hpf, nst), f32)
    for k in range(n - 1, 0, -1):
        new = e_all[k, 0:1, :] * adj + ad_all[k].astype(f32)
        adj = jnp.where(k > c, new, adj)
    g_ref[own_rows, :] = adj
    share(g_ref, 2)

    copy(ob1, ob1r, o_send.at[0], o_recv.at[0], (yn, f)).wait_recv()
    for q in range(outer):
        at = pl.ds(pl.multiple_of((q * 2 + y) * rows_out, 8), rows_out)
        value = ro[at, :] + ob1r[q].astype(f32)
        ro[at, :] = value
        ob2[q] = value.astype(bf16)
    for k in range(1, outer):
        q = lax.rem(z + k, outer)
        start(ob2.at[q], ob2r.at[z], o_send.at[1], o_recv.at[1], (q * 2 + y, f))
    some = pl.ds(0, outer - 1)
    total(ob2.at[some], ob2r.at[some], o_send.at[1], o_recv.at[1])

    merge(0, 2)
    shared(g_ref, 2)
    g2 = split(g_ref[...] * eend)
    gp[hp : 2 * hp, :] = ((dxs + dot3(g2, b2, NN)) * einv).astype(bf16)
    gp[2 * hp : 2 * hp + nst, :] = (db + dot3(transposed(g2), xs2, NN)).astype(bf16)
    rin[hp : 2 * hp + nst, :] = dot1(gp[hp : 2 * hp + nst, :], hid_ref[...], NN)
    to_partner(n_early, n_blocks)
    total(ib1, ib1r, i_send.at[0], iy_recv.at[0])
    merge(2, n_early)

    gpt = gp[...].T
    wi = wi_all[...].reshape(cin, d)
    gh_ref[...] = dot1(gpt, wi, NN).astype(bf16)
    put_gh = pltpu.make_async_copy(gh_ref, gh_any, l_sem.at[6])
    put_gh.start()

    weight = jnp.zeros((1, d), f32)
    for s in range(n):
        w = wo_all[s].astype(f32)
        weight = weight + jnp.sum(w * w, axis=0, keepdims=True)
    w = wi_all[c].astype(f32)
    weight_in = jnp.sum(w * w, axis=1, keepdims=True)

    copy(ob2.at[some], ob2r.at[some], o_send.at[1], o_recv.at[1], (yn, f)).wait_recv()
    acc = ro[pl.ds(pl.multiple_of(c * rows_out, 8), rows_out), :]
    for k in range(1, outer):
        q = lax.rem(z + k, outer)
        acc = acc + ob2r[q].astype(f32)
    acc = acc * (1.0 / root_tokens)
    ro[:rows_out, :] = acc
    nout_out[...] = jnp.sum(acc * acc, axis=0, keepdims=True).reshape(8, d // 8)
    for k in range(1, n):
        start(nout_out, nout_all.at[c], n_send.at[0], n_recv.at[0, c], (lax.rem(c + k, n), f))
    total(nout_all.at[pl.ds(0, n - 1)], nout_all.at[pl.ds(0, n - 1)], n_send.at[0], n_recv.at[0, 0])
    nout_all[c] = nout_out[...]

    merge(n_early, n_blocks)
    sent = n_blocks - rows_in // g
    most = pl.ds(0, sent)
    total(ib2.at[most], ib2.at[most], i_send.at[1], iz_recv.at[0])

    copy(ib2r.at[some], ib2r.at[some], i_send.at[1], iz_recv.at[0], (yn, f)).wait_recv()
    acc = ri[...]
    for k in range(1, outer):
        q = lax.rem(z + k, outer)
        acc = acc + ib2r[q].reshape(rows_in, d).astype(f32)
    acc = acc * (1.0 / root_tokens)
    ri[...] = acc
    at = lax.broadcasted_iota(jnp.int32, (rows_in, 128), 1)
    sums = jnp.where(at < 8, jnp.sum(acc * acc, axis=1, keepdims=True), weight_in)
    nin_out[...] = sums.T[:16, :]
    for k in range(1, fs):
        start(nin_out, nin_all.at[f], n_send.at[1], n_recv.at[1, f], (c, lax.rem(f + k, fs)))
    total(nin_all.at[pl.ds(0, fs - 1)], nin_all.at[pl.ds(0, fs - 1)], n_send.at[1], n_recv.at[1, 0])
    nin_all[f] = nin_out[...]

    grad_square = nout_all[c]
    for k in range(1, n):
        s = lax.rem(c + n - k, n)
        copy(nout_out, nout_all.at[s], n_send.at[0], n_recv.at[0, s], (s, f)).wait_recv()
        grad_square = grad_square + nout_all[s]
    grad_square = grad_square.reshape(1, d)
    factor = jnp.minimum(1.0, clip_output * jnp.maximum(jnp.sqrt(weight), 0.001)
                         / jnp.maximum(jnp.sqrt(grad_square), 1e-06))
    gwo_ref[...] = ro[:rows_out, :] * factor
    put_gwo = pltpu.make_async_copy(gwo_ref, gwo_any, l_sem.at[7])
    put_gwo.start()

    square = nin_all[f]
    for k in range(1, fs):
        p = lax.rem(f + fs - k, fs)
        copy(nin_out, nin_all.at[p], n_send.at[1], n_recv.at[1, p], (c, p)).wait_recv()
        square = square + nin_all[p]
    root = jnp.sqrt(square)
    factor = jnp.minimum(1.0, clip_input * jnp.maximum(root[8:16], 0.001)
                         / jnp.maximum(root[0:8], 1e-06))
    gwi_ref[...] = ri[...] * factor.T[:, 0:1]
    put_gwi = pltpu.make_async_copy(gwi_ref, gwi_any, l_sem.at[8])
    put_gwi.start()

    ins.finish()
    outs.finish()
    for a, (_, ref) in enumerate(both):
        for at in range(outer):
            if at < outer - 1:
                part = ref.at[pl.ds(0, at + 1)]
                total(part, part, g_send.at[0, a], g_recv.at[a, 0], z == at)
            if at > 0:
                part = ref.at[pl.ds(0, outer - at)]
                total(part, part, g_send.at[1, a], g_recv.at[a, 0], z == at)
        part = ref.at[pl.ds(0, outer)]
        total(part, part, g_send.at[2, a], g_recv.at[a, 0])
    for has, args in ends:
        under(has, lambda args=args: copy(*args).wait_send())
    put_gh.wait()
    put_gwo.wait()
    put_gwi.wait()


def one_kernel(n, fs, hidden, w_in, decay, norm_gain, w_out, grad_out):
    tok, d = hidden.shape
    rows_in, rows_out = w_in.shape[0], w_out.shape[0]
    cin, hp = rows_in * n, rows_out * n
    nst = (cin - 2 * hp) // 2
    hpf, outer = hp // fs, n // 2
    hi = rows_in // 2
    g, early, late = early_and_late(n, rows_in, hp, nst)
    per, blocks = rows_in // g, len(early[0]) + len(late[0])
    V = pltpu.VMEM
    dma = pltpu.SemaphoreType.DMA
    scratch = [
        V((d, tok), bf16), V((d, tok), bf16), V((n, rows_in, d), bf16), V((n, rows_out, d), bf16),
        V((cin + hp, tok), f32),
        V((n, rows_in, tok), f32), V((n, hi, tok), f32), V((n, hi, tok), bf16),
        V((n, hi, tok), bf16), V((n, hi, tok), f32),
        V((outer, 2 * rows_out, tok), f32), V((outer, rows_out, tok), f32),
        V((outer, rows_out, tok), bf16), V((outer, rows_out, tok), bf16),
        V((outer, rows_out, tok), f32),
        V((8, nst), f32), V((n, 8, nst), f32),
        V((hp, tok), f32), V((hpf, nst), f32), V((n, hpf, nst), f32), V((hp, nst), f32),
        V((hpf, nst), bf16), V((n, hpf, nst), bf16), V((hp, nst), f32),
        V((hp, d), f32), V((outer, rows_out, d), bf16), V((outer, rows_out, d), bf16),
        V((outer, rows_out, d), bf16), V((outer, rows_out, d), bf16),
        V((cin, tok), bf16), V((cin, d), f32), V((rows_in, d), f32),
        V((blocks, g, d), bf16), V((blocks, g, d), bf16),
        V((blocks, g, d), bf16), V((outer, per, g, d), bf16),
        V((16, rows_in), f32), V((fs, 16, rows_in), f32),
        V((8, d // 8), f32), V((n, 8, d // 8), f32),
        dma((3, 2)), dma((2, n, per)), dma((3,)), dma((3, n)), dma((3,)), dma((3, outer)),
        dma((2, n)), dma((2, n)), dma((3,)), dma((3, n)),
        dma((2,)), dma((2,)), dma((2,)), dma((blocks,)), dma((1,)),
        dma((2,)), dma((2, n)), V((hp, nst), f32),
        V((tok, d), bf16), V((tok, d), bf16), V(decay.shape, f32), V((hp,), f32),
        V((tok, d), bf16), V((rows_in, d), f32), V((rows_out, d), f32), dma((9,)),
    ]
    return pl.pallas_call(
        functools.partial(fused, n, fs, math.sqrt(tok * n), math.sqrt(d * fs)),
        out_shape=(
            V((tok, d), bf16),
            V((rows_in, d), f32),
            V((rows_out, d), f32),
        ),
        in_specs=[pl.BlockSpec(memory_space=pl.ANY)] * 6,
        out_specs=(pl.BlockSpec(memory_space=pl.ANY),) * 3,
        scratch_shapes=scratch,
        compiler_params=pltpu.CompilerParams(
            collective_id=0, has_side_effects=True, vmem_limit_bytes=60 * 1024 * 1024),
    )(hidden, w_in, decay, norm_gain, w_out, grad_out)


def solution(mesh):
    n, fs = mesh.shape["ctx"], mesh.shape["fsdp"]

    def body(hidden, w_in, decay, norm_gain, w_out, grad_out):
        whole_tiles = w_in.shape[0] % 32 == 0 and w_out.shape[0] % 16 == 0 and n % 2 == 0
        if whole_tiles and fs == decay.shape[0] and fs % 2 == 0 and n >= 4 and fits(n, w_in, w_out):
            return one_kernel(n, fs, hidden, w_in, decay, norm_gain, w_out, grad_out)
        return local(hidden, w_in, decay, norm_gain, w_out, grad_out)

    return jax.shard_map(
        body,
        mesh=mesh,
        in_specs=(
            P("ctx", "fsdp"),
            P("ctx", "fsdp"),
            P(None, "ctx"),
            P(),
            P("ctx", "fsdp"),
            P("ctx", "fsdp"),
        ),
        out_specs=(P("ctx", "fsdp"), P("ctx", "fsdp"), P("ctx", "fsdp")),
        check_vma=False,
    )
```

```python
import functools
import math

import jax
import jax.numpy as jnp
from jax import lax
from jax.experimental import pallas as pl
from jax.experimental.pallas import tpu as pltpu
from jax.sharding import PartitionSpec as P

D = 4096
H = 4
P_SIZE = 64
N = 128
HP = 256


highest = lax.Precision.HIGHEST
clip_output = 10.0


def prefix(x, axis, combine, identity):
    count, index = (lax.axis_size(axis), lax.axis_index(axis))
    everything = jax.tree.map(lambda part: lax.all_gather(part, axis), x)
    start = jax.tree.map(
        lambda part, zero: jnp.broadcast_to(jnp.asarray(zero, part.dtype), part.shape), x, identity
    )

    def step(k, before):
        reached = k < index
        new = combine(before, jax.tree.map(lambda part: part[k], everything))
        return jax.tree.map(lambda a, b: jnp.where(reached, a, b), new, before)

    return lax.fori_loop(0, count, step, start)


def entering(x, axis, join, neutral):
    count = lax.axis_size(axis)
    place = lax.axis_index(axis)
    ahead = count - 1 - place
    gathered = jax.tree.map(
        lambda a, kind: lax.all_gather(a.astype(kind), axis),
        x,
        jax.tree.map(lambda a: jnp.bfloat16 if a.dtype == jnp.float32 else a.dtype, x),
    )
    state = jax.tree.map(lambda a, e: jnp.zeros_like(a) + jnp.asarray(e, a.dtype), x, neutral)

    def one(step, state):
        source = count - 1 - step
        return join(
            state,
            jax.tree.map(
                lambda a, own: lax.dynamic_index_in_dim(a, source, 0, False).astype(own.dtype),
                gathered,
                x,
            ),
        )

    return lax.fori_loop(0, ahead, one, state)


def split_columns(projection):
    return (
        projection[:, :HP],
        projection[:, HP : 2 * HP],
        projection[:, 2 * HP : 2 * HP + N],
        projection[:, 2 * HP + N :],
    )


def intra_block(x_part, b_part, c_part, log_decay):
    length = x_part.shape[0]
    cum_decay = jnp.cumsum(log_decay, axis=1)
    x_heads = x_part.reshape(length, H, P_SIZE)
    causal = jnp.arange(length)[:, None] >= jnp.arange(length)[None, :]
    gaps = jnp.where(causal[None], cum_decay[:, :, None] - cum_decay[:, None, :], 0.0)
    weights = jnp.where(causal[None], jnp.exp(gaps), 0.0)
    scores = jnp.dot(c_part, b_part.T, precision=highest)
    mixed = weights * scores[None]
    y_intra = jnp.einsum("hts,shp->thp", mixed, x_heads, precision=highest).reshape(
        length, H * P_SIZE
    )
    tail = jnp.exp(cum_decay[:, -1:] - cum_decay)
    weighted = x_heads * tail.T[:, :, None]
    state_part = jnp.einsum("shp,sn->hpn", weighted, b_part, precision=highest)
    return (y_intra, state_part, cum_decay)


def finish_block(gate_part, y_intra, c_part, start_state, cum_decay, norm_gain):
    length = c_part.shape[0]
    carried = jnp.einsum("hpn,tn->thp", start_state, c_part, precision=highest)
    carried = carried * jnp.exp(cum_decay).T[:, :, None]
    y_full = y_intra + carried.reshape(length, H * P_SIZE)
    gated = y_full * jax.nn.silu(gate_part)
    factor = lax.rsqrt(jnp.mean(gated * gated, axis=-1, keepdims=True) + 1e-05)
    return gated * factor * norm_gain


def carry_states(earlier, later):
    return (earlier[0] * later[0], later[0] * earlier[1] + later[1])


def carry_adjoint(earlier, later):
    return (earlier[0] * later[0], later[1] + later[0] * earlier[1])


def local(hidden, w_in, decay, norm_gain, w_out, grad_out):
    clip_input = math.sqrt(D)
    tok_rows = hidden.shape[0]
    root_tokens = math.sqrt(tok_rows * lax.axis_size("ctx"))
    contract_last = (((1,), (1,)), ((), ()))
    contract_first = (((0,), (0,)), ((), ()))
    partial_proj = lax.dot_general(
        hidden,
        lax.all_gather(w_in, "ctx", axis=0, tiled=True),
        contract_last,
        preferred_element_type=jnp.float32,
    )
    slab_out = lax.all_gather(w_out, "ctx", axis=0, tiled=True)
    partial_grad = lax.dot_general(
        grad_out, slab_out, contract_last, preferred_element_type=jnp.float32
    )
    projection, grad_normed = lax.psum((partial_proj, partial_grad), "fsdp")
    log_decay = jnp.log(decay)
    gate_part, x_part, b_part, c_part = split_columns(projection)

    def intra_only(x_value, b_value, c_value):
        return intra_block(x_value, b_value, c_value, log_decay)

    (y_intra, state_part, cum_decay), intra_pull = jax.vjp(intra_only, x_part, b_part, c_part)
    decay_total = jnp.exp(cum_decay[:, -1])[:, None, None]
    identity = (jnp.ones_like(decay_total), jnp.zeros_like(state_part))
    _, start_state = prefix((decay_total, state_part), "ctx", carry_states, identity)

    def finish_only(gate_value, intra_value, c_value, state_value):
        return finish_block(gate_value, intra_value, c_value, state_value, cum_decay, norm_gain)

    normed, finish_pull = jax.vjp(finish_only, gate_part, y_intra, c_part, start_state)
    grad_gate, grad_intra, grad_c_late, grad_start = finish_pull(grad_normed)
    _, grad_end = entering((decay_total, grad_start), "ctx", carry_adjoint, identity)
    grad_x, grad_b, grad_c_early = intra_pull((grad_intra, grad_end, jnp.zeros_like(cum_decay)))
    grad_projection = jnp.concatenate(
        [grad_gate, grad_x, grad_b, grad_c_early + grad_c_late], axis=1
    ).astype(jnp.bfloat16)
    columns = grad_projection
    grad_hidden = jnp.dot(
        columns, lax.all_gather(w_in, "ctx", axis=0, tiled=True), preferred_element_type=jnp.float32
    )
    columns = grad_projection
    raw_in = (
        lax.psum_scatter(
            lax.dot_general(columns, hidden, contract_first, preferred_element_type=jnp.float32),
            "ctx",
            scatter_dimension=0,
            tiled=True,
        )
        / root_tokens
    )
    weight_square = jnp.sum(jnp.square(w_in.astype(jnp.float32)), axis=1)
    weight_in, grad_in = lax.psum((weight_square, jnp.sum(raw_in * raw_in, axis=1)), "fsdp")
    factor_in = jnp.minimum(
        1.0,
        clip_input
        * jnp.maximum(jnp.sqrt(weight_in), 0.001)
        / jnp.maximum(jnp.sqrt(grad_in), 1e-06),
    )
    normed_rounded = normed.astype(jnp.bfloat16)
    weight_out = jnp.sqrt(jnp.sum(jnp.square(slab_out.astype(jnp.float32)), axis=0))
    raw_out = (
        lax.psum_scatter(
            lax.dot_general(
                normed_rounded, grad_out, contract_first, preferred_element_type=jnp.float32
            ),
            "ctx",
            scatter_dimension=0,
            tiled=True,
        )
        / root_tokens
    )
    grad_square = lax.psum(jnp.sum(raw_out * raw_out, axis=0), "ctx")
    factor_out = jnp.minimum(
        1.0,
        clip_output * jnp.maximum(weight_out, 0.001) / jnp.maximum(jnp.sqrt(grad_square), 1e-06),
    )
    return (
        grad_hidden.astype(jnp.bfloat16),
        raw_in * factor_in[:, None],
        raw_out * factor_out[None, :],
    )


NN = (((1,), (0,)), ((), ()))
NT = (((1,), (1,)), ((), ()))
TN = (((0,), (0,)), ((), ()))
MESH = pl.DeviceIdType.MESH
f32 = jnp.float32
bf16 = jnp.bfloat16
EPS = 1e-05


def split(a):
    hi = a.astype(bf16)
    return hi, (a - hi.astype(f32)).astype(bf16)


def dot1(a, b, dims):
    return lax.dot_general(a, b, dims, preferred_element_type=f32)


def dot3(a, b, dims):
    return dot1(a[0], b[0], dims) + (dot1(a[0], b[1], dims) + dot1(a[1], b[0], dims))


def transposed(pair):
    return pair[0].T, pair[1].T


def early_and_late(n, rows, hp, nst):
    g = math.gcd(rows, math.gcd(hp, nst))
    early, late = [], []
    for y in (0, 1):
        first, last = [], []
        for q in range(n // 2):
            for j in range(rows // g):
                row = (q * 2 + y) * rows + j * g
                soon = row + g <= hp or row >= 2 * hp + nst
                (first if soon else last).append((row, q, j))
        early.append(first)
        late.append(last)
    return g, early, late


def fits(n, w_in, w_out):
    rows, hp = w_in.shape[0], w_out.shape[0] * n
    nst = (rows * n - 2 * hp) // 2
    g, early, late = early_and_late(n, rows, hp, nst)
    same = len(early[0]) == len(early[1]) and len(early[0]) >= 2
    return g % 16 == 0 and same and n % 4 == 0 and w_in.shape[1] % 1024 == 0


def fused(
    n, fs, root_tokens, clip_input,
    hid_any, win_ref, dec_any, gain_any, wout_ref, gout_any,
    gh_any, gwi_any, gwo_any,
    hidT, goutT, wi_all, wo_all, pT,
    bi, ai_in, xi_out, xi_in, ci_in, bo, ao_in, xo_out, xo_in, co_in,
    e_out, e_all, e_ref, st_out, st_all, s0_ref, ad_out, ad_all, g_ref,
    ro, ob1, ob1r, ob2, ob2r, gp, rin, ri, ib1, ib1r, ib2, ib2r, irx,
    nin_out, nin_all, nout_out, nout_all,
    g_send, g_recv, pi_send, pi_recv, po_send, po_recv, s_send, s_recv, t_send, t_recv,
    o_send, o_recv, i_send, iy_recv, iz_recv, ir_recv, n_send, n_recv, tmp,
    hid_ref, gout_ref, dec_ref, gain_ref, gh_ref, gwi_ref, gwo_ref, l_sem,
):
    c = lax.axis_index("ctx")
    f = lax.axis_index("fsdp")
    outer = n // 2
    half = outer // 2
    z, y = c // 2, lax.rem(c, 2)
    yn = c + 1 - 2 * y
    core = lax.rem(f, 2)
    fcore = f + 1 - 2 * core
    fx = lax.rem(f + fs // 2, fs)
    rows_in, d = win_ref.shape
    rows_out = wout_ref.shape[0]
    tok = hid_any.shape[0]
    cin, hp = rows_in * n, rows_out * n
    nst = (cin - 2 * hp) // 2
    hpf = hp // fs
    first = hp // rows_in
    side = z // half
    g, early, late = early_and_late(n, rows_in, hp, nst)

    def copy(src, dst, ssem, rsem, dev):
        return pltpu.make_async_remote_copy(
            src_ref=src, dst_ref=dst, send_sem=ssem, recv_sem=rsem,
            device_id=dev, device_id_type=MESH)

    ends = []

    def under(has, fn, *args):
        if has is None:
            fn(*args)
        else:
            pl.when(has)(lambda: fn(*args))

    def start(*args, when=None):
        under(when, lambda: copy(*args).start())

    def go(*args, when=None):
        start(*args, when=when)
        ends.append((when, args))

    def total(src, dst, sem, rsem, when=None):
        ends.append((when, (src, dst, sem, rsem, (yn, f))))

    local = [
        pltpu.make_async_copy(src, dst, l_sem.at[i])
        for i, (src, dst) in enumerate((
            (hid_any, hid_ref), (win_ref, wi_all.at[c]), (gout_any, gout_ref),
            (wout_ref, wo_all.at[c]), (dec_any, dec_ref), (gain_any, gain_ref)))
    ]
    for each in local:
        each.start()

    barrier = pltpu.get_barrier_semaphore()
    up = jnp.minimum(z + 1, outer - 1) * 2 + y
    down = jnp.maximum(z - 1, 0) * 2 + y
    beside = [(z < outer - 1, (up, f)), (z > 0, (down, f))]
    for has, to in beside + [(None, (yn, f)), (None, (c, fcore)), (None, (c, fx))]:
        under(has, lambda to=to: pl.semaphore_signal(
            barrier, inc=1, device_id=to, device_id_type=MESH))
    pl.semaphore_wait(
        barrier, 3 + jnp.minimum(z, 1) + jnp.minimum(outer - 1 - z, 1))

    both = ((win_ref, wi_all), (wout_ref, wo_all))

    pieces = (rows_in // g, 1)

    def part(ref, a, s, j):
        return ref.at[s] if a else ref.at[s, pl.ds(j * g, g)]

    def own_y():
        start(wout_ref, wo_all.at[c], g_send.at[2, 1], g_recv.at[1, c, 0], (yn, f))

    def own_out():
        for src, s, way in ((wout_ref, c, 0), (wo_all.at[yn], yn, 1)):
            if way:
                landed(1, yn)
            for k in range(outer - 1, 0, -1):
                q = lax.rem(z + k, outer)
                start(src, wo_all.at[s], g_send.at[way, 1], g_recv.at[1, s, 0], (q * 2 + y, f))

    def own_in():
        a = 0
        for j in range(pieces[0]):
            to = part(wi_all, 0, c, j)
            at = win_ref.at[pl.ds(j * g, g)]
            sem = g_recv.at[0, c, j]
            start(at, to, g_send.at[0, a], sem, (up, f), when=z < outer - 1)
            start(at, to, g_send.at[1, a], sem, (down, f), when=z > 0)
            start(at, to, g_send.at[2, a], sem, (yn, f))

    def landed_part(a, s, j):
        at = part(both[a][1], a, s, j)
        copy(at, at, g_send.at[2, a], g_recv.at[a, s, j], (yn, f)).wait_recv()

    def landed(a, s):
        for j in range(pieces[a]):
            landed_part(a, s, j)

    def relay(s, fwd, j):
        at = part(wi_all, 0, s, j)
        has, to, way = fwd
        landed_part(0, s, j)
        start(at, at, g_send.at[way, 0], g_recv.at[0, s, j], (to, f), when=has)

    def cross(a, s, j):
        at = part(both[a][1], a, s, j)
        start(at, at, g_send.at[2, a], g_recv.at[a, s, j], (yn, f))

    own_in()
    own_y()
    for each in local[:2]:
        each.wait()
    hidT[...] = hid_ref[...].T

    hi = rows_in // 2
    mine = pl.ds(pl.multiple_of(core * hi, 8), hi)
    other = pl.ds(pl.multiple_of((1 - core) * hi, 8), hi)
    mine_o = pl.ds(pl.multiple_of(core * rows_out, 8), rows_out)
    other_o = pl.ds(pl.multiple_of((1 - core) * rows_out, 8), rows_out)

    class Chain:
        def __init__(self, part, pair_in, x_out, x_in, back_in, send, recv, mine, other, base):
            self.part, self.pair_in, self.x_out, self.x_in = part, pair_in, x_out, x_in
            self.back_in, self.send, self.recv, self.base = back_in, send, recv, base
            self.mine, self.other, self.half = mine, other, pair_in.shape[1]

        def to_pair(self, s):
            return copy(self.part.at[s, self.other], self.pair_in.at[s], self.send.at[0],
                        self.recv.at[0, s], (c, fcore))

        def across(self, s):
            return copy(self.x_out.at[s], self.x_in.at[s], self.send.at[1],
                        self.recv.at[1, s], (c, fx))

        def back(self, s):
            return copy(self.part.at[s, self.mine], self.back_in.at[s], self.send.at[2],
                        self.recv.at[2, s], (c, fcore))

        def place(self, s, which, value):
            at = self.base + s * (2 * self.half) + which * self.half
            pT[pl.ds(pl.multiple_of(at, 8), self.half), :] = value

        def take(self, s, value):
            self.part[s] = value
            self.to_pair(s).start()

        def pair_sum(self, s):
            self.to_pair(s).wait_recv()
            value = self.part[s, self.mine] + self.pair_in[s]
            self.part[s, self.mine] = value
            self.x_out[s] = value.astype(bf16)
            self.across(s).start()

        def full_sum(self, s):
            self.across(s).wait_recv()
            value = self.part[s, self.mine] + self.x_in[s].astype(f32)
            self.part[s, self.mine] = value
            self.back(s).start()
            self.place(s, core, value)

        def collect(self, s):
            self.back(s).wait_recv()
            self.place(s, 1 - core, self.back_in[s])

        def finish(self):
            total(self.pair_in, self.pair_in, self.send.at[0], self.recv.at[0, 0])
            total(self.x_out, self.x_in, self.send.at[1], self.recv.at[1, 0])
            total(self.back_in, self.back_in, self.send.at[2], self.recv.at[2, 0])

    ins = Chain(bi, ai_in, xi_out, xi_in, ci_in, pi_send, pi_recv, mine, other, 0)
    outs = Chain(bo, ao_in, xo_out, xo_in, co_in, po_send, po_recv, mine_o, other_o, cin)

    def both_true(a, b):
        return b if a is None else jnp.logical_and(a, b)

    def row(k, way):
        there = z - k if way == 0 else z + k
        has = there >= 0 if way == 0 else there < outer
        q = jnp.maximum(there, 0) if way == 0 else jnp.minimum(there, outer - 1)
        fwd = (z < outer - 1, up, 0) if way == 0 else (z > 0, down, 1)
        return has, q, fwd

    def take_in(s):
        ins.take(s, dot1(wi_all[s], hidT[...], NN))

    def soon(has, s):
        return both_true(has, s >= first)

    def ahead(k):
        for j in range(pieces[0]):
            for way in (0, 1):
                has, q, fwd = row(k, way)
                s = q * 2 + y
                under(has, relay, s, fwd, j)
                under(both_true(has, s >= first), cross, 0, s, j)

    def cross_rest():
        for k in range(1, outer):
            for j in range(pieces[0]):
                for way in (0, 1):
                    has, q, _ = row(k, way)
                    s = q * 2 + y
                    under(both_true(has, s < first), cross, 0, s, j)

    def crossed(s):
        landed(0, s)
        take_in(s)

    items, at_stage, lags = [], [0, 0, 0], (3, 7, 11)
    names = ("pair_sum", "full_sum", "collect")

    def settle(stage, upto):
        while at_stage[stage] < upto:
            has, s, chain = items[at_stage[stage]]
            under(has, getattr(chain, names[stage]), s)
            at_stage[stage] += 1

    def feed(has, fn, s, chain, push=True):
        under(has, fn, s)
        items.append((has, s, chain))
        if push:
            for stage, lag in enumerate(lags):
                settle(stage, len(items) - lag)

    def take_gate(s):
        under(lax.rem(s + y, 2) != 0, landed, 0, s)
        take_in(s)

    def take_out(q):
        for s in (q * 2, q * 2 + 1):
            pl.when(q != z)(lambda s=s: landed(1, s))
        at = pl.ds(pl.multiple_of(q * 2, 2), 2)
        outs.take(q, dot1(wo_all[at].reshape(2 * rows_out, d), goutT[...], NN))

    def plane(k):
        for has, q in [(None, z)] if k == 0 else [row(k, way)[:2] for way in (0, 1)]:
            for s in (q * 2, q * 2 + 1):
                feed(both_true(has, s < first), take_gate, s, ins, False)
            feed(has, take_out, q, outs, False)

    def gather():
        feed(soon(None, c), take_in, c, ins)
        later = [(soon(None, yn), yn)]
        for k in range(1, outer):
            ahead(k)
            if k == outer - 1:
                cross_rest()
                own_out()
            for way in (0, 1):
                has, q, _ = row(k, way)
                feed(soon(has, q * 2 + y), take_in, q * 2 + y, ins)
            for has, s in later:
                feed(has, crossed, s, ins)
            later = []
            for way in (0, 1):
                has, q, _ = row(k, way)
                s = q * 2 + 1 - y
                later.append((soon(has, s), s))
        for has, s in later:
            feed(has, crossed, s, ins)
        for stage in range(3):
            settle(stage, len(items))

    def decays():
        decay = dec_ref[...]
        lane = lax.broadcasted_iota(jnp.int32, decay.shape, 1)
        shift = 1
        while shift < tok:
            decay = decay * jnp.where(lane >= shift, pltpu.roll(decay, shift, 1), 1.0)
            shift *= 2
        heads = decay.shape[0]
        for h in range(heads):
            e_ref[h * (hp // heads) : (h + 1) * (hp // heads), :] = jnp.broadcast_to(
                decay[h : h + 1], (hp // heads, tok))
        e_out[...] = jnp.broadcast_to(
            e_ref[pl.ds(pl.multiple_of(f * hpf, 8), 8), tok - 128 : tok][:, 127:128], (8, nst))
        e_all[c] = e_out[...]

    for each in local[2:]:
        each.wait()
    goutT[...] = gout_ref[...].T
    decays()
    gather()

    for k in range(1, n):
        start(e_out, e_all.at[c], t_send.at[0], t_recv.at[0, c], (lax.rem(c + k, n), f))
    total(e_all.at[pl.ds(0, n - 1)], e_all.at[pl.ds(0, n - 1)], t_send.at[0], t_recv.at[0, 0])

    e = e_ref[...]
    einv = 1.0 / e
    eend = e[:, tok - 1 : tok]
    xs = pT[hp : 2 * hp, :] * einv
    bT = pT[2 * hp : 2 * hp + nst, :]
    cT = pT[2 * hp + nst : cin, :]
    xs2, b2, c2 = split(xs), split(bT), split(cT)
    tmp[...] = dot3(xs2, b2, NT) * eend
    own_rows = pl.ds(pl.multiple_of(f * hpf, 8), hpf)
    st_out[...] = tmp[own_rows, :].astype(bf16)
    for k in range(n - 1, 0, -1):
        go(st_out, st_all.at[c], s_send.at[0, k], s_recv.at[0, c],
           (jnp.minimum(c + k, n - 1), f), when=c + k < n)

    upper = lax.broadcasted_iota(jnp.int32, (tok, tok), 0) <= lax.broadcasted_iota(
        jnp.int32, (tok, tok), 1)
    scores2 = split(jnp.where(upper, dot3(transposed(b2), c2, NN), 0.0))
    y_in = dot3(xs2, scores2, NN)
    def share(ref, i):
        for k in range(1, fs):
            start(ref.at[own_rows], ref.at[own_rows], t_send.at[i], t_recv.at[i, f],
                  (c, lax.rem(f + k, fs)))

    def shared(ref, i):
        for k in range(1, fs):
            p = lax.rem(f + fs - k, fs)
            rows = pl.ds(pl.multiple_of(p * hpf, 8), hpf)
            copy(ref.at[rows], ref.at[rows], t_send.at[i], t_recv.at[i, p], (c, p)).wait_recv()

    def start_state():
        for k in range(1, n):
            s = lax.rem(c + n - k, n)
            copy(e_out, e_all.at[s], t_send.at[0], t_recv.at[0, s], (s, f)).wait_recv()
            s = jnp.maximum(c - k, 0)
            pl.when(c - k >= 0)(lambda s=s, k=k: copy(
                st_out, st_all.at[s], s_send.at[0, k], s_recv.at[0, s], (s, f)).wait_recv())
        state = jnp.zeros((hpf, nst), f32)
        for k in range(n - 1):
            new = e_all[k, 0:1, :] * state + st_all[k].astype(f32)
            state = jnp.where(k < c, new, state)
        s0_ref[own_rows, :] = state.astype(bf16)
        share(s0_ref, 1)

    for i in (1, 2):
        some_f = st_all.at[pl.ds(0, fs - 1)]
        total(some_f, some_f, t_send.at[i], t_recv.at[i, 0])
    plane(0)
    plane(1)
    settle(0, len(items))
    soonest = len(items)
    for k in range(2, outer):
        plane(k)
    settle(0, len(items))
    settle(1, soonest)
    start_state()
    settle(1, len(items))

    settle(2, len(items))
    gate = pT[:hp, :]
    sig = 1.0 / (1.0 + jnp.exp(-gate))
    silu = gate * sig

    shared(s0_ref, 1)
    s0 = s0_ref[...]
    yT = (y_in + (dot1(s0, c2[0], NN) + dot1(s0, c2[1], NN))) * e

    gain = jnp.broadcast_to(gain_ref[...].reshape(1, hp), (8, hp)).T[:, 0:1]
    gated = yT * silu
    r = lax.rsqrt(jnp.mean(gated * gated, axis=0, keepdims=True) + EPS)
    normed = (gated * r * gain).astype(bf16)
    u = pT[cin:, :] * gain
    dgated = r * u - gated * (r * r * r * jnp.mean(u * gated, axis=0, keepdims=True))
    dys2 = split(dgated * silu * e)
    tmp[...] = dot3(dys2, c2, NT)
    ad_out[...] = tmp[own_rows, :].astype(bf16)
    for k in range(n - 1, 0, -1):
        go(ad_out, ad_all.at[c], s_send.at[1, k], s_recv.at[1, c],
           (jnp.maximum(c - k, 0), f), when=c - k >= 0)

    blocks = [
        [a + sorted(b, key=lambda block: block[1] if up_side else -block[1])
         for a, b in zip(early, late)]
        for up_side in (0, 1)
    ]
    n_gate = min(sum(b[0] + g <= hp for b in of_y) for of_y in early)
    n_early, n_blocks = len(early[0]), len(blocks[0][0])

    def pick(i, part, to):
        (a, b), (p, q) = [[of_y[i][part] for of_y in of_side] for of_side in blocks]
        return a + to * (b - a) + side * (p - a + to * (q - p - b + a))

    def to_partner(lo, hi):
        for i in range(lo, hi):
            at = pl.ds(pl.multiple_of(pick(i, 0, 1 - y), 8), g)
            ib1[i] = rin[at, :].astype(bf16)
            start(ib1.at[i], ib1r.at[i], i_send.at[0], iy_recv.at[i], (yn, f))

    near = half - 1 + side
    is_near = z == near

    def place_of(i):
        q, j = pick(i, 1, y), pick(i, 2, y)
        return pl.ds(pl.multiple_of(pick(i, 0, y), 8), g), q, j, q // half != side

    def onward(i, value, q, j):
        ib2[i] = value.astype(bf16)
        copy(ib2.at[i], ib2r.at[z, j], i_send.at[1], iz_recv.at[0], (q * 2 + y, f)).start()

    def merge_one(i):
        copy(ib1.at[i], ib1r.at[i], i_send.at[0], iy_recv.at[i], (yn, f)).wait_recv()
        at, q, j, cross = place_of(i)
        value = rin[at, :] + ib1r[i].astype(f32)

        def keep():
            ri[pl.ds(pl.multiple_of(j * g, 8), g), :] = value

        def hold():
            rin[at, :] = value

        def hand():
            ib2[i] = value.astype(bf16)
            slot = z - side * (half + 1)
            copy(ib2.at[i], irx.at[slot, i], i_send.at[1], ir_recv.at[slot, i],
                 (near * 2 + y, f)).start()

        stay = jnp.logical_not(cross)
        pl.when(q == z)(keep)
        pl.when(jnp.logical_and(stay, q != z))(lambda: onward(i, value, q, j))
        pl.when(jnp.logical_and(cross, is_near))(hold)
        if half > 1:
            pl.when(jnp.logical_and(cross, jnp.logical_not(is_near)))(hand)

    def cross_one(i):
        at, q, j, cross = place_of(i)

        def add():
            value = rin[at, :]
            for slot in range(half - 1):
                copy(ib2.at[i], irx.at[slot, i], i_send.at[1], ir_recv.at[slot, i],
                     (yn, f)).wait_recv()
                value = value + irx[slot, i].astype(f32)
            onward(i, value, q, j)

        pl.when(jnp.logical_and(cross, is_near))(add)

    def merge(lo, hi):
        for i in range(lo, hi):
            merge_one(i)
            if i >= 3:
                cross_one(i - 3)
        if hi == n_blocks:
            for i in range(max(hi - 3, 0), hi):
                cross_one(i)

    gp[:hp, :] = (dgated * yT * (sig * (1.0 + gate * (1.0 - sig)))).astype(bf16)
    rin[:hp, :] = dot1(gp[:hp, :], hid_ref[...], NN)
    to_partner(0, n_gate)
    ro[...] = dot1(normed, gout_ref[...], NN)
    for q in range(outer):
        ob1[q] = ro[q * 2 * rows_out : (q + 1) * 2 * rows_out, :].astype(bf16)
    for k in range(outer - 1, 0, -1):
        q = lax.rem(z + k, outer)
        start(ob1.at[q], ob1r.at[z], o_send.at[0], o_recv.at[0], (q * 2 + y, f))
    some = pl.ds(0, outer - 1)
    total(ob1.at[some], ob1r.at[some], o_send.at[0], o_recv.at[0])

    dscores = jnp.where(upper, dot1(xs2[0].T, dys2[0], NN), 0.0).astype(bf16)
    gp[2 * hp + nst :, :] = (dot1(b2[0], dscores, NN) + dot1(s0.T, dys2[0], NN)).astype(bf16)
    rin[2 * hp + nst :, :] = dot1(gp[2 * hp + nst :, :], hid_ref[...], NN)
    to_partner(n_gate, n_early)
    db = dot1(c2[0], dscores, NT)
    dxs = dot1(dys2[0], scores2[0], NT)

    for k in range(1, n):
        s = jnp.minimum(c + k, n - 1)
        pl.when(c + k < n)(lambda s=s, k=k: copy(
            ad_out, ad_all.at[s], s_send.at[1, k], s_recv.at[1, s], (s, f)).wait_recv())
    adj = jnp.zeros((hpf, nst), f32)
    for k in range(n - 1, 0, -1):
        new = e_all[k, 0:1, :] * adj + ad_all[k].astype(f32)
        adj = jnp.where(k > c, new, adj)
    g_ref[own_rows, :] = adj.astype(bf16)
    share(g_ref, 2)

    merge(0, 2)
    shared(g_ref, 2)
    g2 = split(g_ref[...].astype(f32) * eend)
    gp[hp : 2 * hp, :] = ((dxs + dot3(g2, b2, NN)) * einv).astype(bf16)
    gp[2 * hp : 2 * hp + nst, :] = (db + dot3(transposed(g2), xs2, NN)).astype(bf16)
    rin[hp : 2 * hp + nst, :] = dot1(gp[hp : 2 * hp + nst, :], hid_ref[...], NN)
    to_partner(n_early, n_blocks)
    total(ib1, ib1r, i_send.at[0], iy_recv.at[0])
    merge(2, n_early)

    late_on = max(n_blocks - 3, n_early)
    merge(n_early, late_on)
    copy(ob1.at[some], ob1r.at[some], o_send.at[0], o_recv.at[0], (yn, f)).wait_recv()

    def plane_sum(side_y):
        at = pl.ds(pl.multiple_of((z * 2 + side_y) * rows_out, 8), rows_out)
        from_y = pl.ds(pl.multiple_of(side_y * rows_out, 8), rows_out)
        value = ro[at, :]
        for k in range(1, outer):
            value = value + ob1r[lax.rem(z + k, outer), from_y, :].astype(f32)
        return value

    ob2[...] = plane_sum(1 - y).astype(bf16)
    go(ob2, ob2r, o_send.at[1], o_recv.at[1], (yn, f))
    out_part = plane_sum(y)
    merge(late_on, n_blocks)
    copy(ob2, ob2r, o_send.at[1], o_recv.at[1], (yn, f)).wait_recv()
    acc = out_part + ob2r[...].astype(f32)
    acc = acc * (1.0 / root_tokens)
    ro[:rows_out, :] = acc
    nout_out[...] = jnp.sum(acc * acc, axis=0, keepdims=True).reshape(8, d // 8)
    for k in range(1, n):
        start(nout_out, nout_all.at[c], n_send.at[0], n_recv.at[0, c], (lax.rem(c + k, n), f))
    total(nout_all.at[pl.ds(0, n - 1)], nout_all.at[pl.ds(0, n - 1)], n_send.at[0], n_recv.at[0, 0])
    nout_all[c] = nout_out[...]

    sent = n_blocks - rows_in // g
    most = pl.ds(0, sent)
    total(ib2.at[most], ib2.at[most], i_send.at[1], iz_recv.at[0])

    gpt = gp[...].T
    wi = wi_all[...].reshape(cin, d)
    gh_ref[...] = dot1(gpt, wi, NN).astype(bf16)
    put_gh = pltpu.make_async_copy(gh_ref, gh_any, l_sem.at[6])
    put_gh.start()

    weight = jnp.zeros((1, d), f32)
    for s in range(n):
        w = wo_all[s].astype(f32)
        weight = weight + jnp.sum(w * w, axis=0, keepdims=True)
    w = wi_all[c].astype(f32)
    weight_in = jnp.sum(w * w, axis=1, keepdims=True)

    full = ib2r.at[pl.ds(0, half)]
    copy(full, full, i_send.at[1], iz_recv.at[0], (yn, f)).wait_recv()
    acc = ri[...]
    for k in range(1, half):
        q = side * half + lax.rem(z - side * half + k, half)
        acc = acc + ib2r[q].reshape(rows_in, d).astype(f32)
    acc = acc + ib2r[half - side].reshape(rows_in, d).astype(f32)
    acc = acc * (1.0 / root_tokens)
    ri[...] = acc
    at = lax.broadcasted_iota(jnp.int32, (rows_in, 128), 1)
    sums = jnp.where(at < 8, jnp.sum(acc * acc, axis=1, keepdims=True), weight_in)
    nin_out[...] = sums.T[:16, :]
    for k in range(1, fs):
        start(nin_out, nin_all.at[f], n_send.at[1], n_recv.at[1, f], (c, lax.rem(f + k, fs)))
    total(nin_all.at[pl.ds(0, fs - 1)], nin_all.at[pl.ds(0, fs - 1)], n_send.at[1], n_recv.at[1, 0])
    nin_all[f] = nin_out[...]

    grad_square = nout_all[c]
    for k in range(1, n):
        s = lax.rem(c + n - k, n)
        copy(nout_out, nout_all.at[s], n_send.at[0], n_recv.at[0, s], (s, f)).wait_recv()
        grad_square = grad_square + nout_all[s]
    grad_square = grad_square.reshape(1, d)
    factor = jnp.minimum(1.0, clip_output * jnp.maximum(jnp.sqrt(weight), 0.001)
                         / jnp.maximum(jnp.sqrt(grad_square), 1e-06))
    gwo_ref[...] = ro[:rows_out, :] * factor
    put_gwo = pltpu.make_async_copy(gwo_ref, gwo_any, l_sem.at[7])
    put_gwo.start()

    square = nin_all[f]
    for k in range(1, fs):
        p = lax.rem(f + fs - k, fs)
        copy(nin_out, nin_all.at[p], n_send.at[1], n_recv.at[1, p], (c, p)).wait_recv()
        square = square + nin_all[p]
    root = jnp.sqrt(square)
    factor = jnp.minimum(1.0, clip_input * jnp.maximum(root[8:16], 0.001)
                         / jnp.maximum(root[0:8], 1e-06))
    gwi_ref[...] = ri[...] * factor.T[:, 0:1]
    put_gwi = pltpu.make_async_copy(gwi_ref, gwi_any, l_sem.at[8])
    put_gwi.start()

    ins.finish()
    outs.finish()
    for at in range(outer):
        if at < outer - 1:
            part_up = wi_all.at[pl.ds(0, at + 1)]
            total(part_up, part_up, g_send.at[0, 0], g_recv.at[0, 0, 0], z == at)
        if at > 0:
            part_down = wi_all.at[pl.ds(0, outer - at)]
            total(part_down, part_down, g_send.at[1, 0], g_recv.at[0, 0, 0], z == at)
    part_y = wi_all.at[pl.ds(0, outer)]
    total(part_y, part_y, g_send.at[2, 0], g_recv.at[0, 0, 0])
    part_z = wo_all.at[pl.ds(0, outer - 1)]
    for way in (0, 1):
        total(part_z, part_z, g_send.at[way, 1], g_recv.at[1, 0, 0])
    total(wo_all.at[0], wo_all.at[0], g_send.at[2, 1], g_recv.at[1, 0, 0])
    for has, args in ends:
        under(has, lambda args=args: copy(*args).wait_send())
    put_gh.wait()
    put_gwo.wait()
    put_gwi.wait()


def write_out(a_ref, b_ref, c_ref, ao_ref, bo_ref, co_ref, sem):
    copies = [
        pltpu.make_async_copy(src, dst, sem.at[i])
        for i, (src, dst) in enumerate(((a_ref, ao_ref), (b_ref, bo_ref), (c_ref, co_ref)))
    ]
    for each in copies:
        each.start()
    for each in copies:
        each.wait()


def one_kernel(n, fs, hidden, w_in, decay, norm_gain, w_out, grad_out):
    tok, d = hidden.shape
    rows_in, rows_out = w_in.shape[0], w_out.shape[0]
    cin, hp = rows_in * n, rows_out * n
    nst = (cin - 2 * hp) // 2
    hpf, outer = hp // fs, n // 2
    hi = rows_in // 2
    g, early, late = early_and_late(n, rows_in, hp, nst)
    per, blocks = rows_in // g, len(early[0]) + len(late[0])
    V = pltpu.VMEM
    dma = pltpu.SemaphoreType.DMA
    scratch = [
        V((d, tok), bf16), V((d, tok), bf16), V((n, rows_in, d), bf16), V((n, rows_out, d), bf16),
        V((cin + hp, tok), f32),
        V((n, rows_in, tok), f32), V((n, hi, tok), f32), V((n, hi, tok), bf16),
        V((n, hi, tok), bf16), V((n, hi, tok), f32),
        V((outer, 2 * rows_out, tok), f32), V((outer, rows_out, tok), f32),
        V((outer, rows_out, tok), bf16), V((outer, rows_out, tok), bf16),
        V((outer, rows_out, tok), f32),
        V((8, nst), f32), V((n, 8, nst), f32),
        V((hp, tok), f32), V((hpf, nst), bf16), V((n, hpf, nst), bf16), V((hp, nst), bf16),
        V((hpf, nst), bf16), V((n, hpf, nst), bf16), V((hp, nst), bf16),
        V((hp, d), f32), V((outer, 2 * rows_out, d), bf16), V((outer, 2 * rows_out, d), bf16),
        V((rows_out, d), bf16), V((rows_out, d), bf16),
        V((cin, tok), bf16), V((cin, d), f32), V((rows_in, d), f32),
        V((blocks, g, d), bf16), V((blocks, g, d), bf16),
        V((blocks, g, d), bf16), V((outer, per, g, d), bf16),
        V((max(outer // 2 - 1, 1), blocks, g, d), bf16),
        V((16, rows_in), f32), V((fs, 16, rows_in), f32),
        V((8, d // 8), f32), V((n, 8, d // 8), f32),
        dma((3, 2)), dma((2, n, per)), dma((3,)), dma((3, n)), dma((3,)), dma((3, outer)),
        dma((2, n)), dma((2, n)), dma((3,)), dma((3, n)),
        dma((2,)), dma((2,)), dma((2,)), dma((blocks,)), dma((1,)),
        dma((max(outer // 2 - 1, 1), blocks)),
        dma((2,)), dma((2, n)), V((hp, nst), f32),
        V((tok, d), bf16), V((tok, d), bf16), V(decay.shape, f32), V((hp,), f32),
        V((tok, d), bf16), V((rows_in, d), f32), V((rows_out, d), f32), dma((9,)),
    ]
    outs = pl.pallas_call(
        functools.partial(fused, n, fs, math.sqrt(tok * n), math.sqrt(d * fs)),
        out_shape=(
            V((tok, d), bf16),
            V((rows_in, d), f32),
            V((rows_out, d), f32),
        ),
        in_specs=[pl.BlockSpec(memory_space=pl.ANY)] * 6,
        out_specs=(pl.BlockSpec(memory_space=pl.ANY),) * 3,
        scratch_shapes=scratch,
        compiler_params=pltpu.CompilerParams(
            collective_id=0, has_side_effects=True, vmem_limit_bytes=60 * 1024 * 1024),
    )(hidden, w_in, decay, norm_gain, w_out, grad_out)
    return pl.pallas_call(
        write_out,
        out_shape=tuple(jax.ShapeDtypeStruct(o.shape, o.dtype) for o in outs),
        in_specs=[pl.BlockSpec(memory_space=pltpu.VMEM)] * 3,
        out_specs=(pl.BlockSpec(memory_space=pl.ANY),) * 3,
        scratch_shapes=[dma((3,))],
    )(*[pltpu.with_memory_space_constraint(o, pltpu.VMEM) for o in outs])


def solution(mesh):
    n, fs = mesh.shape["ctx"], mesh.shape["fsdp"]

    def body(hidden, w_in, decay, norm_gain, w_out, grad_out):
        whole_tiles = w_in.shape[0] % 32 == 0 and w_out.shape[0] % 16 == 0 and n % 2 == 0
        if whole_tiles and fs == decay.shape[0] and fs % 2 == 0 and n >= 4 and fits(n, w_in, w_out):
            return one_kernel(n, fs, hidden, w_in, decay, norm_gain, w_out, grad_out)
        return local(hidden, w_in, decay, norm_gain, w_out, grad_out)

    return jax.shard_map(
        body,
        mesh=mesh,
        in_specs=(
            P("ctx", "fsdp"),
            P("ctx", "fsdp"),
            P(None, "ctx"),
            P(),
            P("ctx", "fsdp"),
            P("ctx", "fsdp"),
        ),
        out_specs=(P("ctx", "fsdp"), P("ctx", "fsdp"), P("ctx", "fsdp")),
        check_vma=False,
    )
```
